32 devices in a mesh: fsdp: 4 (over x, core), ctx: 4 (over z), tp: 2 (over y).
Axes of the slice: x: 2, y: 2, z: 4, core: 2. Of those that a mesh axis runs over, the one named last changes fastest.
Arguments:
- tokens: bfloat16 [8, 1024, 2048], P('fsdp', ('ctx', 'tp')), may hold values from -6 to 6
- side_input: bfloat16 [8, 1024, 256], P('fsdp', ('ctx', 'tp')), may hold values from -6 to 6
- prefix: int32 [8], P('fsdp'), may hold values from 102 to 512
- positions: int32 [8, 1024], P('fsdp', 'ctx'), may hold values from 0 to 2046, as said below
- cotangent: bfloat16 [8, 1024, 2048], P('fsdp', ('ctx', 'tp')), may hold values from -6 to 6
- query_weight: bfloat16 [2048, 2048], P(('fsdp', 'ctx'), 'tp'), may hold values from -0.125 to 0.125
- key_matrix: bfloat16 [2048, 512], P(('fsdp', 'ctx'), 'tp'), may hold values from -0.125 to 0.125
- value_matrix: bfloat16 [2048, 512], P(('fsdp', 'ctx'), 'tp'), may hold values from -0.125 to 0.125
- out_weight: bfloat16 [2048, 2048], P('tp', ('fsdp', 'ctx')), may hold values from -0.125 to 0.125
- gate_weight: bfloat16 [2048, 8192], P(('fsdp', 'ctx'), 'tp'), may hold values from -0.125 to 0.125
- up_weight: bfloat16 [2048, 8192], P(('fsdp', 'ctx'), 'tp'), may hold values from -0.125 to 0.125
- down_weight: bfloat16 [8192, 2048], P('tp', ('fsdp', 'ctx')), may hold values from -0.0625 to 0.0625
- laurel_left: bfloat16 [2048, 64], P(('fsdp', 'ctx', 'tp')), may hold values from -0.125 to 0.125
- laurel_right: bfloat16 [64, 2048], P(None, ('fsdp', 'ctx', 'tp')), may hold values from -0.75 to 0.75
- side_gate_weight: bfloat16 [2048, 256], P(('fsdp', 'ctx', 'tp')), may hold values from -0.125 to 0.125
- side_out_weight: bfloat16 [256, 2048], P(None, ('fsdp', 'ctx', 'tp')), may hold values from -0.375 to 0.375
- input_gain: float32 [2048], replicated, may hold values from 0.25 to 1.75
- laurel_gain: float32 [2048], replicated, may hold values from 0.25 to 1.75
- attention_gain: float32 [2048], replicated, may hold values from 0.25 to 1.75
- hidden_in_gain: float32 [2048], replicated, may hold values from 0.25 to 1.75
- hidden_out_gain: float32 [2048], replicated, may hold values from 0.25 to 1.75
- side_gain: float32 [2048], replicated, may hold values from 0.25 to 1.75
- query_gain: float32 [256], replicated, may hold values from 0.08 to 0.18
- key_gain: float32 [256], replicated, may hold values from 0.5 to 1.5
Outputs:
- output: bfloat16 [8, 1024, 2048], P('fsdp', ('ctx', 'tp'))
- tokens_grad: float32 [8, 1024, 2048], P('fsdp', ('ctx', 'tp'))
- side_input_grad: float32 [8, 1024, 256], P('fsdp', ('ctx', 'tp'))
- query_weight_grad: float32 [2048, 2048], P(('fsdp', 'ctx'), 'tp')
- key_weight_grad: float32 [2048, 512], P(('fsdp', 'ctx'), 'tp')
- value_weight_grad: float32 [2048, 512], P(('fsdp', 'ctx'), 'tp')
- out_weight_grad: float32 [2048, 2048], P('tp', ('fsdp', 'ctx'))
- gate_weight_grad: float32 [2048, 8192], P(('fsdp', 'ctx'), 'tp')
- up_weight_grad: float32 [2048, 8192], P(('fsdp', 'ctx'), 'tp')
- down_weight_grad: float32 [8192, 2048], P('tp', ('fsdp', 'ctx'))
- laurel_left_grad: float32 [2048, 64], P(('fsdp', 'ctx', 'tp'))
- laurel_right_grad: float32 [64, 2048], P(None, ('fsdp', 'ctx', 'tp'))
- side_gate_weight_grad: float32 [2048, 256], P(('fsdp', 'ctx', 'tp'))
- side_out_weight_grad: float32 [256, 2048], P(None, ('fsdp', 'ctx', 'tp'))
- input_gain_grad: float32 [2048], replicated
- laurel_gain_grad: float32 [2048], replicated
- attention_gain_grad: float32 [2048], replicated
- hidden_in_gain_grad: float32 [2048], replicated
- hidden_out_gain_grad: float32 [2048], replicated
- side_gain_grad: float32 [2048], replicated
- query_gain_grad: float32 [256], replicated
- key_gain_grad: float32 [256], replicated
The draws below stay inside these ranges and needn't reach their ends.
Inputs may be any that keep to these rules, and one draw needn't show every extreme that they name: The first prefix[b] tokens of sequence b see one another in both directions. Within each sequence positions rise strictly, from 0 at the first token to 2046 at the last.
All inputs are finite; a program needn't handle non-finite values.
Results may differ from the reference program's by a relative error of at most 0.022.
Values may be sent and summed in bfloat16 or wider, within the bound.
No kernel may reach another device: no remote copies, remote signals or barrier semaphores. Data moves between devices by JAX's collectives and lax.ppermute only.
A program may use at most 320 MiB of HBM per device.

```python
import math
import jax
import jax.numpy as jnp
from jax import lax

MODEL_WIDTH = 2048
QUERY_HEADS = 8
KEY_VALUE_HEADS = 2
HEAD_SIZE = 256
FF = 8192
RANK = 64
PLE = 256
SEQ_LEN = 1024
SEQS = 8


def draw_positions(key, part):
    flips = jax.random.randint(key, (SEQS, SEQ_LEN), 0, 2).astype(jnp.int32)
    index = jnp.arange(SEQ_LEN, dtype=jnp.int32)
    inner = (index > 0) & (index < SEQ_LEN - 1)
    flips = jnp.where(inner[None, :], flips, 0)
    return (2 * index[None, :] - flips).astype(jnp.int32)


def set_ends(entries, rng, least, high):
    place = [jax.random.randint(jax.random.fold_in(rng, axis), (), 0, length) for axis, length in enumerate(entries.shape)]
    widest = entries.shape.index(max(entries.shape))
    beside = place[:widest] + [(place[widest] + 1) % entries.shape[widest]] + place[widest + 1:]
    return entries.at[tuple(place)].set(least).at[tuple(beside)].set(high)


def levels(rng, shape, cuts, smallest, largest):
    def one(axis_at, shards_of):
        steps = jax.random.uniform(jax.random.fold_in(jax.random.fold_in(rng, 6), axis_at), (shards_of,), jnp.float32, smallest / len(cuts), largest / len(cuts))
        return jnp.repeat(jnp.exp(steps), shape[axis_at] // shards_of).reshape((-1,) + (1,) * (len(shape) - axis_at - 1))

    level = one(*cuts[0])
    for cut in cuts[1:]:
        level = level * one(*cut)
    return level


def normal_values(key, shape, spread, most, split=(), kind=jnp.bfloat16):
    array = jax.random.normal(key, shape, jnp.float32) * spread
    if len(split) > 0:
        array = levels(key, shape, split, -0.22, 0.18) * array
    return jnp.clip(array, min=-most, max=most).astype(kind)


def setup_inputs(seed: int = 0) -> dict:
    key_of = jax.random.split(jax.random.key(seed), 25)
    tokens = normal_values(key_of[0], (SEQS, SEQ_LEN, MODEL_WIDTH), 1.0, 6.0, ((0, 4), (1, 8)))
    side_input = normal_values(key_of[1], (SEQS, SEQ_LEN, PLE), 1.0, 6.0, ((0, 4), (1, 8)))
    prefix = set_ends(jax.random.randint(key_of[2], (SEQS,), SEQ_LEN // 10, SEQ_LEN // 2 + 1), jax.random.fold_in(key_of[2], 1), SEQ_LEN // 10, (SEQ_LEN // 2 + 1) - 1).astype(jnp.int32)
    positions = draw_positions(jax.random.fold_in(key_of[24], 71), 0)
    cotangent = normal_values(key_of[4], (SEQS, SEQ_LEN, MODEL_WIDTH), 1.0, 6.0, ((0, 4), (1, 8)))
    query_weight = normal_values(key_of[5], (MODEL_WIDTH, QUERY_HEADS * HEAD_SIZE), MODEL_WIDTH ** -0.5, 0.125, ((0, 16), (1, 2)))
    key_matrix = normal_values(key_of[6], (MODEL_WIDTH, KEY_VALUE_HEADS * HEAD_SIZE), MODEL_WIDTH ** -0.5, 0.125, ((0, 16), (1, 2)))
    value_matrix = normal_values(key_of[7], (MODEL_WIDTH, KEY_VALUE_HEADS * HEAD_SIZE), MODEL_WIDTH ** -0.5, 0.125, ((0, 16), (1, 2)))
    out_weight = normal_values(key_of[8], (QUERY_HEADS * HEAD_SIZE, MODEL_WIDTH), (QUERY_HEADS * HEAD_SIZE) ** -0.5, 0.125, ((0, 2), (1, 16)))
    gate_weight = normal_values(key_of[9], (MODEL_WIDTH, FF), MODEL_WIDTH ** -0.5, 0.125, ((0, 16), (1, 2)))
    up_weight = normal_values(key_of[10], (MODEL_WIDTH, FF), MODEL_WIDTH ** -0.5, 0.125, ((0, 16), (1, 2)))
    down_weight = normal_values(key_of[11], (FF, MODEL_WIDTH), FF ** -0.5, 0.0625, ((0, 2), (1, 16)))
    laurel_left = normal_values(key_of[12], (MODEL_WIDTH, RANK), MODEL_WIDTH ** -0.5, 0.125, ((0, 32),))
    laurel_right = normal_values(key_of[13], (RANK, MODEL_WIDTH), RANK ** -0.5, 0.75, ((1, 32),))
    side_gate_weight = normal_values(key_of[14], (MODEL_WIDTH, PLE), MODEL_WIDTH ** -0.5, 0.125, ((0, 32),))
    side_out_weight = normal_values(key_of[15], (PLE, MODEL_WIDTH), PLE ** -0.5, 0.375, ((1, 32),))
    input_gain = jnp.clip(1.0 + 0.15 * jax.random.normal(key_of[16], (MODEL_WIDTH,), jnp.float32), 0.25, 1.75)
    laurel_gain = jnp.clip(1.0 + 0.15 * jax.random.normal(key_of[17], (MODEL_WIDTH,), jnp.float32), 0.25, 1.75)
    attention_gain = jnp.clip(1.0 + 0.15 * jax.random.normal(key_of[18], (MODEL_WIDTH,), jnp.float32), 0.25, 1.75)
    hidden_in_gain = jnp.clip(1.0 + 0.15 * jax.random.normal(key_of[19], (MODEL_WIDTH,), jnp.float32), 0.25, 1.75)
    hidden_out_gain = jnp.clip(1.0 + 0.15 * jax.random.normal(key_of[20], (MODEL_WIDTH,), jnp.float32), 0.25, 1.75)
    side_gain = jnp.clip(1.0 + 0.15 * jax.random.normal(key_of[21], (MODEL_WIDTH,), jnp.float32), 0.25, 1.75)
    query_gain = jnp.clip(jnp.exp(jax.random.uniform(key_of[22], (HEAD_SIZE,), jnp.float32, math.log(0.08), math.log(0.18))), 0.08, 0.18)
    key_gain = jnp.clip(1.0 + 0.1 * jax.random.normal(key_of[23], (HEAD_SIZE,), jnp.float32), 0.5, 1.5)
    return {"tokens": tokens, "side_input": side_input, "prefix": prefix, "positions": positions, "cotangent": cotangent, "query_weight": query_weight, "key_matrix": key_matrix, "value_matrix": value_matrix, "out_weight": out_weight, "gate_weight": gate_weight, "up_weight": up_weight, "down_weight": down_weight, "laurel_left": laurel_left, "laurel_right": laurel_right, "side_gate_weight": side_gate_weight, "side_out_weight": side_out_weight, "input_gain": input_gain, "laurel_gain": laurel_gain, "attention_gain": attention_gain, "hidden_in_gain": hidden_in_gain, "hidden_out_gain": hidden_out_gain, "side_gain": side_gain, "query_gain": query_gain, "key_gain": key_gain}


EPS = 1e-06
THETA = 1000000.0
MASKED = -1e+30
SQRT_HALF = 0.7071067811865476

@jax.custom_vjp
def low(v):
    return lax.optimization_barrier(v.astype(jnp.bfloat16)).astype(jnp.float32)

@jax.custom_vjp
def reduced_backward(v):
    return v

def low_keep(v):
    return (low(v), None)

def low_pass(kept, grad):
    return (grad,)

def back_keep(v):
    return (v, None)

def back_low(kept, grad):
    return (low(grad),)
low.defvjp(low_keep, low_pass)
reduced_backward.defvjp(back_keep, back_low)

def product_result(left, right):
    return jnp.dot(left, right, precision=lax.Precision.HIGHEST, preferred_element_type=jnp.float32)

def scaled_norm(value, gain):
    return value * lax.rsqrt(lax.optimization_barrier(jnp.mean(value * value, axis=-1, keepdims=True)) + EPS) * gain

def plain_norm(value):
    return value * lax.rsqrt(lax.optimization_barrier(jnp.mean(value * value, axis=-1, keepdims=True)) + EPS)

def rotate(value, positions):
    half = value.shape[-1] // 2
    freq = THETA ** (-(jnp.arange(half, dtype=jnp.float32) * 2.0) / value.shape[-1])
    angle = positions.astype(jnp.float32)[..., None] * freq
    cosine = jnp.cos(angle)[..., None, :]
    sine = jnp.sin(angle)[..., None, :]
    first = value[..., :half]
    second = value[..., half:]
    return jnp.concatenate([first * cosine - second * sine, second * cosine + first * sine], axis=-1)

def geglu(gate, upward):
    return jax.nn.gelu(gate, approximate=True) * upward

def attend(query_rows, keys, values, prefix):
    length_total = query_rows.shape[0]
    head_groups = QUERY_HEADS // KEY_VALUE_HEADS
    block_slice = min(512, length_total)
    query_block_list = query_rows.reshape(length_total // block_slice, block_slice, KEY_VALUE_HEADS, head_groups, HEAD_SIZE)
    starts = (jnp.arange(length_total // block_slice) * block_slice).astype(jnp.int32)
    key_index = jnp.arange(length_total).astype(jnp.int32)

    def one_block(item):
        query_part, start = item
        scores = reduced_backward(jnp.einsum('bkgd,jkd->kgbj', query_part, keys, precision=lax.Precision.HIGHEST))
        rows = start + jnp.arange(block_slice).astype(jnp.int32)
        visible = (key_index[None, :] <= rows[:, None]) | (key_index[None, :] < prefix)
        scores = jnp.where(visible, scores, MASKED)
        weights = low(jax.nn.softmax(scores, axis=-1))
        return jnp.einsum('kgbj,jkd->bkgd', weights, values, precision=lax.Precision.HIGHEST)
    outputs = lax.map(jax.checkpoint(one_block), (query_block_list, starts))
    return outputs.reshape(length_total, QUERY_HEADS * HEAD_SIZE)

def forward(params, inputs, side_values, prefix, positions):
    query_weight, key_matrix, value_matrix, out_weight, gate_weight, up_weight, down_weight, laurel_left, laurel_right, side_gate_weight, side_out_weight, input_gain, laurel_gain, attention_gain, hidden_in_gain, hidden_out_gain, side_gain, query_gain, key_gain = params
    length_total = inputs.shape[0]
    normed = scaled_norm(inputs, input_gain)
    normed_reduced = low(normed)
    query_raw = reduced_backward(product_result(normed_reduced, query_weight)).reshape(length_total, QUERY_HEADS, HEAD_SIZE)
    key_unrotated = reduced_backward(product_result(normed_reduced, key_matrix)).reshape(length_total, KEY_VALUE_HEADS, HEAD_SIZE)
    value_unprojected = reduced_backward(product_result(normed_reduced, value_matrix)).reshape(length_total, KEY_VALUE_HEADS, HEAD_SIZE)
    query_rows = low(rotate(scaled_norm(query_raw, query_gain), positions))
    keys = low(rotate(scaled_norm(key_unrotated, key_gain), positions))
    values = low(plain_norm(value_unprojected))
    attended = low(reduced_backward(attend(query_rows, keys, values, prefix)))
    attention = reduced_backward(product_result(attended, out_weight))
    laurel_mid = low(reduced_backward(product_result(normed_reduced, laurel_left)))
    laurel_out = reduced_backward(product_result(laurel_mid, laurel_right))
    mixed = (inputs + scaled_norm(attention, attention_gain) + normed + scaled_norm(laurel_out, laurel_gain)) * SQRT_HALF
    hidden_in = low(scaled_norm(mixed, hidden_in_gain))
    gate = reduced_backward(product_result(hidden_in, gate_weight))
    upward = reduced_backward(product_result(hidden_in, up_weight))
    hidden = low(geglu(gate, upward))
    hidden_out = reduced_backward(product_result(hidden, down_weight))
    layer_out = mixed + scaled_norm(hidden_out, hidden_out_gain)
    layer_low = low(layer_out)
    side_pre = reduced_backward(product_result(layer_low, side_gate_weight))
    side_act = low(geglu(side_pre, side_values))
    projected = reduced_backward(product_result(side_act, side_out_weight))
    return layer_out + scaled_norm(projected, side_gain)

def reference(tokens, side_input, prefix, positions, cotangent, query_weight, key_matrix, value_matrix, out_weight, gate_weight, up_weight, down_weight, laurel_left, laurel_right, side_gate_weight, side_out_weight, input_gain, laurel_gain, attention_gain, hidden_in_gain, hidden_out_gain, side_gain, query_gain, key_gain):
    params = tuple((entry.astype(jnp.float32) for entry in (query_weight, key_matrix, value_matrix, out_weight, gate_weight, up_weight, down_weight, laurel_left, laurel_right, side_gate_weight, side_out_weight, input_gain, laurel_gain, attention_gain, hidden_in_gain, hidden_out_gain, side_gain, query_gain, key_gain)))

    def one_sequence(totals, entry):
        inputs, side_values, span, places, upstream = entry

        def runner(weights, values, side_part):
            return forward(weights, values, side_part, span, places)
        result, pullback = jax.vjp(runner, params, inputs.astype(jnp.float32), side_values.astype(jnp.float32))
        param_grads, input_grads, side_grads = pullback(upstream.astype(jnp.float32))
        totals = jax.tree.map(lambda summed, update: summed + update, totals, param_grads)
        return (totals, (result.astype(jnp.bfloat16), input_grads, side_grads))
    zeros = jax.tree.map(jnp.zeros_like, params)
    totals, (outputs, tokens_grad, side_input_grad) = lax.scan(one_sequence, zeros, (tokens, side_input, prefix, positions, cotangent))
    return (outputs, tokens_grad, side_input_grad, totals[0], totals[1], totals[2], totals[3], totals[4], totals[5], totals[6], totals[7], totals[8], totals[9], totals[10], totals[11], totals[12], totals[13], totals[14], totals[15], totals[16], totals[17], totals[18])
```

```python
import jax
import jax.numpy as jnp
from jax import lax
from jax.sharding import PartitionSpec as P

HEAD_SIZE = 256


EPS = 1e-06
THETA = 1000000.0
MASKED = -1e30
SQRT_HALF = 0.7071067811865476


def scaled_norm(value, gain):
    return value * lax.rsqrt(jnp.mean(value * value, axis=-1, keepdims=True) + EPS) * gain


def plain_norm(value):
    return value * lax.rsqrt(jnp.mean(value * value, axis=-1, keepdims=True) + EPS)


def rotate(value, positions):
    half = value.shape[-1] // 2
    freq = THETA ** (-(jnp.arange(half, dtype=jnp.float32) * 2.0) / value.shape[-1])
    angle = positions.astype(jnp.float32)[..., None] * freq
    cosine = jnp.cos(angle)[..., None, :]
    sine = jnp.sin(angle)[..., None, :]
    first = value[..., :half]
    second = value[..., half:]
    return jnp.concatenate(
        [first * cosine - second * sine, second * cosine + first * sine], axis=-1
    )


def geglu(gate, upward):
    return jax.nn.gelu(gate, approximate=True) * upward


def attention_mix(inputs, attention, normed, laurel, attention_gain, laurel_gain):
    return (
        inputs + scaled_norm(attention, attention_gain) + normed + scaled_norm(laurel, laurel_gain)
    ) * SQRT_HALF


def residual_mix(residual, branch, gain):
    return residual + scaled_norm(branch, gain)


def matmul(left, right):
    return jnp.dot(left, right, preferred_element_type=jnp.float32)


def matmul_t(left, right):
    return lax.dot_general(
        left, right, (((1,), (1,)), ((), ())), preferred_element_type=jnp.float32
    )


def low(value):
    return value.astype(jnp.bfloat16)


def wide(value):
    return value.astype(jnp.float32)


def core_swap(value):
    size = lax.axis_size("fsdp")
    return lax.ppermute(value, "fsdp", [(i, i ^ 1) for i in range(size)])


def x_shift(value, step=1):
    size = lax.axis_size("fsdp")
    return lax.ppermute(value, "fsdp", [(i, (i + 2 * step) % size) for i in range(size)])


def z_shift(value, step=1):
    size = lax.axis_size("ctx")
    return lax.ppermute(value, "ctx", [(i, (i + step) % size) for i in range(size)])


def y_swap(value):
    return lax.ppermute(value, "tp", [(0, 1), (1, 0)])


def by_core(core, mine, other, axis):
    first = jnp.where(core == 0, mine, other)
    second = jnp.where(core == 0, other, mine)
    return jnp.stack([first, second], axis)


class Place:
    def __init__(self):
        self.chips = lax.axis_size("fsdp") // 2
        self.depth = lax.axis_size("ctx")
        index = lax.axis_index("fsdp")
        self.core = index % 2
        self.x = index // 2
        self.z = lax.axis_index("ctx")
        self.y = lax.axis_index("tp")

    def source(self, dx, dz):
        return (self.x - dx) % self.chips, (self.z - dz) % self.depth


def gather_pieces(place, shard):
    pieces = {(0, 0): shard}
    for dz in range(1, place.depth):
        pieces[0, dz] = z_shift(pieces[0, dz - 1])
    for dz in range(place.depth):
        for dx in range(1, place.chips):
            pieces[dx, dz] = x_shift(pieces[dx - 1, dz])
    return pieces


def assemble(place, pieces, cores):
    piece = pieces[0, 0]
    if cores:
        whole = jnp.zeros((place.chips, 2, place.depth) + piece.shape[1:], piece.dtype)
    else:
        whole = jnp.zeros((place.chips, place.depth) + piece.shape, piece.dtype)
    for (dx, dz), piece in pieces.items():
        x, z = place.source(dx, dz)
        if cores:
            whole = lax.dynamic_update_slice(whole, piece[None, :, None], (x, 0, z, 0, 0))
        else:
            whole = lax.dynamic_update_slice(whole, piece[None, None], (x, z, 0, 0))
    return whole


def scatter_pieces(place, partial):
    passing = None
    for step in range(1, place.depth + 1):
        dz = step % place.depth
        arrived = None
        for dx in range(1, place.chips):
            value = partial(dx, dz)
            if arrived is not None:
                value = value + wide(arrived)
            arrived = x_shift(low(value))
        value = partial(0, dz)
        if arrived is not None:
            value = value + wide(arrived)
        if passing is not None:
            value = value + wide(passing)
        if dz == 0:
            return value
        passing = z_shift(low(value))


def sum_everywhere(place, value):
    value = value + core_swap(value)
    value = value + y_swap(value)
    value = sum([x_shift(value, step) for step in range(1, place.chips)], value)
    return sum([z_shift(value, step) for step in range(1, place.depth)], value)


def split_core(place, shard):
    rows, columns = shard.shape
    halves = shard.reshape(rows, 2, columns // 2)
    kept = lax.dynamic_index_in_dim(halves, place.core, 1, False)
    sent = lax.dynamic_index_in_dim(halves, 1 - place.core, 1, False)
    return by_core(place.core, kept, core_swap(sent), 0)


def join_core(place, value):
    kept = lax.dynamic_index_in_dim(value, place.core, 0, False)
    sent = lax.dynamic_index_in_dim(value, 1 - place.core, 0, False)
    both = by_core(place.core, kept, core_swap(sent), 1)
    return both.reshape(both.shape[0], -1)


def share_four(value):
    pair = jnp.concatenate([value, y_swap(value)], 0)
    return jnp.concatenate([pair, core_swap(pair)], 0)


def sum_four(value):
    rows = value.shape[0] // 4
    pair = value[: 2 * rows] + wide(core_swap(low(value[2 * rows :])))
    return pair[:rows] + wide(y_swap(low(pair[rows:])))


def share_two(value):
    return jnp.concatenate([value, y_swap(value)], 1)


def sum_two(value):
    rows = value.shape[1] // 2
    return value[:, :rows] + wide(y_swap(low(value[:, rows:])))


def columns_of(place, value, dx, dz, core, rows):
    x, z = place.source(dx, dz)
    start = ((x * 2 + core) * place.depth + z) * rows
    return lax.dynamic_slice_in_dim(value, start, rows, 1)


def on_device(
    tokens,
    side_input,
    prefix,
    positions,
    cotangent,
    query_weight,
    key_matrix,
    value_matrix,
    out_weight,
    gate_weight,
    up_weight,
    down_weight,
    laurel_left,
    laurel_right,
    side_gate_weight,
    side_out_weight,
    input_gain,
    laurel_gain,
    attention_gain,
    hidden_in_gain,
    hidden_out_gain,
    side_gain,
    query_gain,
    key_gain,
):
    place = Place()
    chips, depth = place.chips, place.depth
    sequences, own_rows, width = tokens.shape
    side_width = side_input.shape[2]
    rank = laurel_left.shape[1]
    block_rows = positions.shape[1]
    shard_rows = query_weight.shape[0]
    query_width = query_weight.shape[1]
    key_width = key_matrix.shape[1]
    hidden_half = gate_weight.shape[1] // 2
    local_heads = query_width // HEAD_SIZE
    local_groups = key_width // HEAD_SIZE
    per_group = local_heads // local_groups

    near = place.y * own_rows + jnp.arange(own_rows, dtype=jnp.int32)
    far = (1 - place.y) * own_rows + jnp.arange(own_rows, dtype=jnp.int32)
    block_index = jnp.concatenate([near, far])
    row_index = place.z * block_rows + block_index
    near_positions = lax.dynamic_slice_in_dim(positions, place.y * own_rows, own_rows, 1)
    far_positions = lax.dynamic_slice_in_dim(positions, (1 - place.y) * own_rows, own_rows, 1)
    positions = jnp.concatenate([near_positions, far_positions], 1)

    mixed_shard = jnp.concatenate([query_weight, key_matrix, value_matrix], 1)
    half = assemble(place, gather_pieces(place, mixed_shard), False)
    mixed_full = by_core(place.core, half, core_swap(half), 1).reshape(width, -1)
    half = assemble(place, gather_pieces(place, out_weight.T), False)
    out_full = by_core(place.core, half, core_swap(half), 1).reshape(width, query_width)

    small = jnp.concatenate(
        [laurel_left, laurel_right.T, side_gate_weight, side_out_weight.T], 1
    )
    small_rows = small.shape[0]
    small = jnp.where(
        place.y == 0,
        jnp.concatenate([small, y_swap(small)], 0),
        jnp.concatenate([y_swap(small), small], 0),
    )
    half = assemble(place, gather_pieces(place, small), False)
    small_full = by_core(place.core, half, core_swap(half), 1).reshape(width, -1)
    laurel_down = small_full[:, :rank]
    laurel_up_t = small_full[:, rank : 2 * rank]
    side_gate_full = small_full[:, 2 * rank : 2 * rank + side_width]
    side_out_t = small_full[:, 2 * rank + side_width :]

    gate_up = jnp.concatenate(
        [split_core(place, gate_weight), split_core(place, up_weight)], 2
    )
    gate_up_full = assemble(place, gather_pieces(place, gate_up), True).reshape(width, -1)
    down_t = split_core(place, down_weight.T)
    down_full_t = assemble(place, gather_pieces(place, down_t), True).reshape(width, -1)

    inputs = tokens.astype(jnp.float32)
    normed, input_pull = jax.vjp(scaled_norm, inputs, input_gain)
    normed_reduced = normed.astype(jnp.bfloat16)
    flat_in = share_two(normed_reduced).reshape(-1, width)
    mixed_raw = matmul(flat_in, mixed_full)
    query_raw = mixed_raw[:, :query_width]
    key_unrotated = mixed_raw[:, query_width : query_width + key_width]
    value_unprojected = mixed_raw[:, query_width + key_width :]

    def heads_of(query_part, key_part, value_part, gain_query, gain_key):
        rotated_queries = rotate(
            scaled_norm(
                query_part.reshape(sequences, block_rows, local_heads, HEAD_SIZE), gain_query
            ),
            positions,
        )
        rotated_keys = rotate(
            scaled_norm(key_part.reshape(sequences, block_rows, local_groups, HEAD_SIZE), gain_key),
            positions,
        )
        normed_values = plain_norm(
            value_part.reshape(sequences, block_rows, local_groups, HEAD_SIZE)
        )
        return (rotated_queries, rotated_keys, normed_values)

    (query_rows, keys, values), heads_pull = jax.vjp(
        heads_of, query_raw, key_unrotated, value_unprojected, query_gain, key_gain
    )
    query_low = query_rows.astype(jnp.bfloat16).reshape(
        sequences, block_rows, local_groups, per_group, HEAD_SIZE
    )
    both = jnp.concatenate([low(keys), low(values)], 2)
    pieces = [both]
    for dz in range(1, depth):
        pieces.append(z_shift(pieces[-1]))
    key_index = jnp.concatenate(
        [((place.z - dz) % depth) * block_rows + block_index for dz in range(depth)]
    )
    everyone = jnp.concatenate(pieces, 1)
    all_keys = everyone[:, :, :local_groups]
    all_values = everyone[:, :, local_groups:]
    visible = (key_index[None, None, :] <= row_index[None, :, None]) | (
        key_index[None, None, :] < prefix[:, None, None]
    )

    def all_scores():
        scores = jnp.einsum(
            "sbkgd,sjkd->skgbj", query_low, all_keys, preferred_element_type=jnp.float32
        )
        return jnp.where(visible[:, None, None], scores, MASKED)

    scores = all_scores()
    highest = jnp.max(scores, axis=-1, keepdims=True)
    log_total = highest + jnp.log(jnp.sum(jnp.exp(scores - highest), axis=-1, keepdims=True))
    probs = jnp.exp(scores - log_total)
    probs_low = low(probs)
    attended = jnp.einsum(
        "skgbj,sjkd->sbkgd", probs_low, all_values, preferred_element_type=jnp.float32
    )
    attended_low = attended.astype(jnp.bfloat16).reshape(
        sequences * block_rows, local_heads * HEAD_SIZE
    )
    attention = sum_two(matmul_t(attended_low, out_full).reshape(sequences, block_rows, width))
    flat_normed = normed_reduced.reshape(-1, width)
    laurel_mid = matmul(flat_normed, laurel_down).astype(jnp.bfloat16)
    laurel_out = matmul_t(laurel_mid, laurel_up_t).reshape(sequences, own_rows, width)
    mixed, mix_pull = jax.vjp(
        attention_mix, inputs, attention, normed, laurel_out, attention_gain, laurel_gain
    )
    hidden_in, pre_pull = jax.vjp(scaled_norm, mixed, hidden_in_gain)
    hidden_block = share_four(low(hidden_in).reshape(-1, width))
    gate_up_out = matmul(hidden_block, gate_up_full)
    hidden, hidden_pull = jax.vjp(
        geglu, gate_up_out[:, :hidden_half], gate_up_out[:, hidden_half:]
    )
    hidden_low = low(hidden)
    hidden_out = sum_four(matmul_t(hidden_low, down_full_t)).reshape(inputs.shape)
    layer_out, post_pull = jax.vjp(residual_mix, mixed, hidden_out, hidden_out_gain)
    layer_low = layer_out.astype(jnp.bfloat16).reshape(-1, width)
    side_pre = matmul(layer_low, side_gate_full)
    side_act, side_pull = jax.vjp(
        geglu, side_pre, side_input.astype(jnp.float32).reshape(-1, side_width)
    )
    side_low = side_act.astype(jnp.bfloat16)
    projected = matmul_t(side_low, side_out_t).reshape(sequences, own_rows, width)
    result, final_pull = jax.vjp(residual_mix, layer_out, projected, side_gain)
    out_grad_first, projected_grad, side_gain_grad = final_pull(cotangent.astype(jnp.float32))
    projected_low = projected_grad.astype(jnp.bfloat16).reshape(-1, width)
    side_out_grad_t = matmul(projected_low.T, side_low)
    side_grad = matmul(projected_low, side_out_t)
    side_pre_grad, side_input_grad = side_pull(side_grad)
    side_pre_low = side_pre_grad.astype(jnp.bfloat16)
    side_gate_grad = matmul(layer_low.T, side_pre_low)
    layer_grad = out_grad_first + matmul_t(side_pre_low, side_gate_full).reshape(inputs.shape)
    mixed_grad_first, hidden_out_grad, hidden_out_gain_grad = post_pull(layer_grad)
    hidden_out_block = share_four(low(hidden_out_grad).reshape(-1, width))

    def cores_columns(value, dx, dz):
        return jnp.concatenate(
            [columns_of(place, value, dx, dz, core, shard_rows) for core in range(2)], 1
        )

    down_grad_t = join_core(
        place,
        scatter_pieces(
            place, lambda dx, dz: matmul(cores_columns(hidden_out_block, dx, dz).T, hidden_low)
        ).reshape(2, shard_rows, -1),
    )
    hidden_grad = matmul(hidden_out_block, down_full_t)
    gate_grad_full, up_grad_full = hidden_pull(hidden_grad)
    gate_up_low = jnp.concatenate([low(gate_grad_full), low(up_grad_full)], 1)
    gate_up_grad = scatter_pieces(
        place, lambda dx, dz: matmul(cores_columns(hidden_block, dx, dz).T, gate_up_low)
    ).reshape(2, shard_rows, -1)
    gate_grad = join_core(place, gate_up_grad[:, :, :hidden_half])
    up_grad = join_core(place, gate_up_grad[:, :, hidden_half:])
    hidden_in_sum = sum_four(matmul_t(gate_up_low, gate_up_full)).reshape(inputs.shape)
    mixed_grad_second, hidden_in_gain_grad = pre_pull(hidden_in_sum)
    mixed_grad = mixed_grad_first + mixed_grad_second
    (
        inputs_grad_first,
        attention_grad,
        normed_grad_first,
        laurel_grad,
        attention_gain_grad,
        laurel_gain_grad,
    ) = mix_pull(mixed_grad)
    attention_block = share_two(low(attention_grad)).reshape(-1, width)

    def scatter_attention(left, right):
        def rows(core, dx, dz):
            return columns_of(place, left, dx, dz, core, shard_rows)

        order = [(dx, dz) for dz in range(depth) for dx in range(chips)]
        sent = jnp.concatenate([rows(1 - place.core, dx, dz) for dx, dz in order], 1)
        arrived = core_swap(low(matmul(sent.T, right)))
        arrived = arrived.reshape(len(order), shard_rows, right.shape[1])
        return scatter_pieces(
            place,
            lambda dx, dz: matmul(rows(place.core, dx, dz).T, right)
            + wide(arrived[order.index((dx, dz))]),
        )

    out_grad_t = scatter_attention(attention_block, attended_low)
    attended_grad = (
        matmul(attention_block, out_full)
        .astype(jnp.bfloat16)
        .reshape(sequences, block_rows, local_groups, per_group, HEAD_SIZE)
    )
    laurel_low = laurel_grad.astype(jnp.bfloat16).reshape(-1, width)
    laurel_right_grad_t = matmul(laurel_low.T, laurel_mid)
    laurel_mid_grad = matmul(laurel_low, laurel_up_t).astype(jnp.bfloat16)
    laurel_left_grad = matmul(flat_normed.T, laurel_mid_grad)
    normed_grad_second = matmul_t(laurel_mid_grad, laurel_down).reshape(inputs.shape)

    def scatter_small(value):
        value = value.reshape(chips, 2, depth, 2 * small_rows, -1)
        kept = lax.dynamic_index_in_dim(value, place.core, 1, False)
        sent = lax.dynamic_index_in_dim(value, 1 - place.core, 1, False)
        value = kept + wide(core_swap(low(sent)))

        def partial(dx, dz):
            x, z = place.source(dx, dz)
            return lax.dynamic_slice(
                value, (x, z, 0, 0), (1, 1) + value.shape[2:]
            ).reshape(value.shape[2:])

        own = scatter_pieces(place, partial).reshape(2, small_rows, -1)
        kept = lax.dynamic_index_in_dim(own, place.y, 0, False)
        sent = lax.dynamic_index_in_dim(own, 1 - place.y, 0, False)
        return kept + wide(y_swap(low(sent)))

    side_grads = scatter_small(jnp.concatenate([side_gate_grad, side_out_grad_t], 1))
    laurel_grads = scatter_small(jnp.concatenate([laurel_left_grad, laurel_right_grad_t], 1))

    delta = jnp.transpose(
        jnp.sum(attended_grad.astype(jnp.float32) * attended, axis=-1), (0, 2, 3, 1)
    )
    probs = jnp.exp(all_scores() - log_total)
    probs_grad = jnp.einsum(
        "sbkgd,sjkd->skgbj", attended_grad, all_values, preferred_element_type=jnp.float32
    )
    scores_grad = low(probs * (probs_grad - delta[..., None]))
    query_grad = jnp.einsum(
        "skgbj,sjkd->sbkgd", scores_grad, all_keys, preferred_element_type=jnp.float32
    )
    keys_grad = jnp.einsum(
        "skgbj,sbkgd->sjkd", scores_grad, query_low, preferred_element_type=jnp.float32
    )
    values_grad = jnp.einsum(
        "skgbj,sbkgd->sjkd", low(probs), attended_grad, preferred_element_type=jnp.float32
    )
    both_grad = jnp.concatenate([keys_grad, values_grad], 2)
    passing = None
    for step in range(1, depth + 1):
        dz = step % depth
        value = both_grad[:, dz * block_rows : (dz + 1) * block_rows]
        if passing is not None:
            value = value + wide(passing)
        if dz:
            passing = z_shift(low(value))
    query_raw_grad, key_raw_grad, value_raw_grad, query_gain_grad, key_gain_grad = heads_pull(
        (
            query_grad.reshape(sequences, block_rows, local_heads, HEAD_SIZE),
            value[:, :, :local_groups],
            value[:, :, local_groups:],
        )
    )
    mixed_low = jnp.concatenate(
        [low(query_raw_grad), low(key_raw_grad), low(value_raw_grad)], 1
    )
    mixed_weight_grad = scatter_attention(flat_in, mixed_low)
    block_in_grad = matmul_t(mixed_low, mixed_full).reshape(sequences, block_rows, width)
    normed_grad = normed_grad_first + normed_grad_second + sum_two(block_in_grad)
    inputs_grad_second, input_gain_grad = input_pull(normed_grad)
    tokens_grad = inputs_grad_first + inputs_grad_second
    early = sum_everywhere(
        place,
        jnp.stack(
            [
                laurel_gain_grad,
                attention_gain_grad,
                hidden_in_gain_grad,
                hidden_out_gain_grad,
                side_gain_grad,
            ]
        ),
    )
    late = sum_everywhere(
        place, jnp.concatenate([input_gain_grad, query_gain_grad, key_gain_grad])
    )
    gain_grads = (late[:width],) + tuple(early) + (
        late[width : width + HEAD_SIZE],
        late[width + HEAD_SIZE :],
    )
    side_input_grad = side_input_grad.reshape(sequences, own_rows, side_width)
    return (
        (result.astype(jnp.bfloat16), tokens_grad, side_input_grad)
        + (
            mixed_weight_grad[:, :query_width],
            mixed_weight_grad[:, query_width : query_width + key_width],
            mixed_weight_grad[:, query_width + key_width :],
            out_grad_t.T,
            gate_grad,
            up_grad,
            down_grad_t.T,
        )
        + (
            laurel_grads[:, :rank],
            laurel_grads[:, rank:].T,
            side_grads[:, :side_width],
            side_grads[:, side_width:].T,
        )
        + gain_grads
    )


def solution(mesh):
    placed = (
        P("fsdp", ("ctx", "tp"), None),
        P("fsdp", ("ctx", "tp"), None),
        P("fsdp"),
        P("fsdp", "ctx"),
        P("fsdp", ("ctx", "tp"), None),
        P(("fsdp", "ctx"), "tp"),
        P(("fsdp", "ctx"), "tp"),
        P(("fsdp", "ctx"), "tp"),
        P("tp", ("fsdp", "ctx")),
        P(("fsdp", "ctx"), "tp"),
        P(("fsdp", "ctx"), "tp"),
        P("tp", ("fsdp", "ctx")),
        P(("fsdp", "ctx", "tp"), None),
        P(None, ("fsdp", "ctx", "tp")),
        P(("fsdp", "ctx", "tp"), None),
        P(None, ("fsdp", "ctx", "tp")),
        P(),
        P(),
        P(),
        P(),
        P(),
        P(),
        P(),
        P(),
    )
    return jax.shard_map(
        on_device,
        mesh=mesh,
        in_specs=placed,
        out_specs=(
            P("fsdp", ("ctx", "tp"), None),
            P("fsdp", ("ctx", "tp"), None),
            P("fsdp", ("ctx", "tp"), None),
            P(("fsdp", "ctx"), "tp"),
            P(("fsdp", "ctx"), "tp"),
            P(("fsdp", "ctx"), "tp"),
            P("tp", ("fsdp", "ctx")),
            P(("fsdp", "ctx"), "tp"),
            P(("fsdp", "ctx"), "tp"),
            P("tp", ("fsdp", "ctx")),
            P(("fsdp", "ctx", "tp"), None),
            P(None, ("fsdp", "ctx", "tp")),
            P(("fsdp", "ctx", "tp"), None),
            P(None, ("fsdp", "ctx", "tp")),
            P(),
            P(),
            P(),
            P(),
            P(),
            P(),
            P(),
            P(),
        ),
        check_vma=False,
    )
```

```python
import jax
import jax.numpy as jnp
from jax import lax
from jax.experimental import pallas as pl
from jax.experimental.pallas import tpu as pltpu
from jax.sharding import Mesh, PartitionSpec as P

HEAD_SIZE = 256


EPS = 1e-06
THETA = 1000000.0
MASKED = -1e30
SQRT_HALF = 0.7071067811865476
LANES = 128


def scaled_norm(value, gain):
    return value * lax.rsqrt(jnp.mean(value * value, axis=-1, keepdims=True) + EPS) * gain


def plain_norm(value):
    return value * lax.rsqrt(jnp.mean(value * value, axis=-1, keepdims=True) + EPS)


def rotate(value, cosine, sine):
    half = value.shape[-1] // 2
    first = value[..., :half]
    second = value[..., half:]
    return jnp.concatenate(
        [first * cosine - second * sine, second * cosine + first * sine], axis=-1
    )


def geglu(gate, upward):
    return jax.nn.gelu(gate, approximate=True) * upward


def attention_mix(inputs, attention, normed, laurel, attention_gain, laurel_gain):
    return (
        inputs + scaled_norm(attention, attention_gain) + normed + scaled_norm(laurel, laurel_gain)
    ) * SQRT_HALF


def residual_mix(residual, branch, gain):
    return residual + scaled_norm(branch, gain)


def matmul(left, right):
    return jnp.dot(left, right, preferred_element_type=jnp.float32)


def matmul_t(left, right):
    return lax.dot_general(
        left, right, (((1,), (1,)), ((), ())), preferred_element_type=jnp.float32
    )


def low(value):
    return value.astype(jnp.bfloat16)


def wide(value):
    return value.astype(jnp.float32)


def tie(*values):
    return lax.optimization_barrier(values)


CTX = ("pair", "odd")


def core_swap(value):
    return lax.ppermute(value, "core", [(0, 1), (1, 0)])


def x_shift(value, step=1):
    size = lax.axis_size("x")
    return lax.ppermute(value, "x", [(i, (i + step) % size) for i in range(size)])


def z_shift(value, step=1):
    size = lax.axis_size(CTX)
    return lax.ppermute(value, CTX, [(i, (i + step) % size) for i in range(size)])


def pair_shift(value):
    size = lax.axis_size("pair")
    return lax.ppermute(value, "pair", [(i, (i + 1) % size) for i in range(size)])


def odd_swap(value):
    return lax.ppermute(value, "odd", [(0, 1), (1, 0)])


def y_swap(value):
    return lax.ppermute(value, "tp", [(0, 1), (1, 0)])


def in_order(own, mine, other, axis):
    first = jnp.where(own == 0, mine, other)
    second = jnp.where(own == 0, other, mine)
    return jnp.stack([first, second], axis)


def halves_of(value, axis, own):
    shape = value.shape
    value = value.reshape(shape[:axis] + (2, shape[axis] // 2) + shape[axis + 1 :])
    kept = lax.dynamic_index_in_dim(value, own, axis, False)
    return kept, lax.dynamic_index_in_dim(value, 1 - own, axis, False)


class Place:
    def __init__(self, rows):
        self.rows = rows
        self.chips = chips = lax.axis_size("x")
        self.pairs = pairs = lax.axis_size("pair")
        self.depth = depth = 2 * pairs
        self.core = core = lax.axis_index("core")
        self.x = x = lax.axis_index("x")
        self.y = lax.axis_index("tp")
        self.pair = pair = lax.axis_index("pair")
        self.odd = lax.axis_index("odd")
        self.z = z = pair * 2 + self.odd
        count = 2 * chips * depth

        def whole(xs, cores, zs):
            return (xs * 2 + cores) * depth + zs

        def near(xs, cores, zs):
            return (((core + cores) % 2) * chips + (x - xs) % chips) * depth + (z - zs) % depth

        at = jnp.arange(count, dtype=jnp.int32)
        of_whole = (at // (2 * depth), (at // depth) % 2, at % depth)
        of_near = (
            (x - (at // depth) % chips) % chips,
            (core + at // (chips * depth)) % 2,
            (z - at) % depth,
        )
        self.whole_to_near = whole(*of_near).astype(jnp.int32)
        self.near_to_whole = near(*of_whole).astype(jnp.int32)

    def move(self, value, index):
        rows = self.rows
        if rows % LANES:
            shape = value.shape
            value = value.reshape(shape[0], -1, rows)
            return jnp.take(value, index, axis=1).reshape(shape)

        def kernel(index_ref, value_ref, out_ref):
            for i in range(value.shape[1] // rows):
                start = pl.multiple_of(index_ref[i] * rows, LANES)
                out_ref[:, i * rows : (i + 1) * rows] = value_ref[:, pl.ds(start, rows)]

        return pl.pallas_call(
            kernel,
            out_shape=jax.ShapeDtypeStruct(value.shape, value.dtype),
            in_specs=[
                pl.BlockSpec(memory_space=pltpu.SMEM),
                pl.BlockSpec(memory_space=pltpu.VMEM),
            ],
            out_specs=pl.BlockSpec(memory_space=pltpu.VMEM),
            name="move_blocks",
        )(index, value)


def z_ring(place, shard):
    ring = [shard]
    for _ in range(1, place.depth):
        ring.append(z_shift(ring[-1]))
    return ring


def rows_of(place, columns):
    return jnp.concatenate(
        [column[dx] for dx in range(place.chips) for column in columns], 0
    )


def scatter_x(place, partial, splits):
    rows = place.rows
    parts = {}
    for first, last in splits:
        run = None
        for dx in range(1, place.chips):
            value = partial(dx, first, last)
            if run is not None:
                value = value + wide(run)
            run = x_shift(low(value))
        value = partial(0, first, last)
        if run is not None:
            value = value + wide(run)
        for dz in range(first, last):
            parts[dz] = value[(dz - first) * rows : (dz - first + 1) * rows]
    return parts


def scatter_z(place, parts):
    passing = None
    for step in range(1, place.depth):
        value = parts[step]
        if passing is not None:
            value = value + wide(passing)
        passing = z_shift(low(value))
    return parts[0] + wide(passing)


def sum_everywhere(place, value):
    value = value + core_swap(value)
    value = value + y_swap(value)
    value = sum([x_shift(value, step) for step in range(1, place.chips)], value)
    return sum([z_shift(value, step) for step in range(1, place.depth)], value)


def swap_middle(place, value, first):
    second = 2 * place.pairs // first
    size = 2 * place.rows
    return jnp.concatenate(
        [
            value[:, ((x * first + a) * second + b) * size :][:, :size]
            for x in range(place.chips)
            for b in range(second)
            for a in range(first)
        ],
        1,
    )


def to_fixed(place, value):
    return swap_middle(place, value, 2)


def from_fixed(place, value):
    return swap_middle(place, value, place.pairs)


def take(value, index, axis):
    return lax.dynamic_index_in_dim(value, index, axis, False)


def quarters(place, shards):
    return jnp.concatenate([shard.reshape(place.rows, 2, 2, -1) for shard in shards], 3)


def join_four(place, value, parts):
    rows = place.rows
    value = value.reshape(2, 2, rows, -1)
    kept = lax.dynamic_index_in_dim(value, place.odd, 1, False)
    sent = lax.dynamic_index_in_dim(value, 1 - place.odd, 1, False)
    value = in_order(place.odd, kept, wide(odd_swap(low(sent))), 2)
    kept = lax.dynamic_index_in_dim(value, place.core, 0, False)
    sent = lax.dynamic_index_in_dim(value, 1 - place.core, 0, False)
    value = in_order(place.core, kept, core_swap(sent), 1)
    return [part.reshape(rows, -1) for part in jnp.split(value, parts, 3)]


def x_ring(place, piece):
    pieces = [piece]
    for _ in range(1, place.chips):
        pieces.append(x_shift(pieces[-1]))
    return pieces


def share_four(value):
    half = value.shape[0] // 2
    beside = y_swap(value)
    above = odd_swap(value)
    across = [y_swap(above[:half]), odd_swap(beside[half:])]
    return jnp.concatenate([value, beside, above] + across, 0)


def add_core(value):
    return jnp.concatenate([value, core_swap(value)], 0)


def sum_across(value, arrived, product):
    rows = value.shape[0] // 8
    half = rows // 2

    def own(first, last):
        return product(value[first:last]) + wide(arrived[first:last])

    across = low(own(3 * rows, 4 * rows))
    above_half = y_swap(across[:half])
    beside_half = odd_swap(across[half:])
    beside_first = y_swap(low(own(rows, rows + half)))
    above_last = odd_swap(low(own(2 * rows + half, 3 * rows)))
    return own, across, above_half, beside_half, beside_first, above_last


def sum_beside(rows, own, above_half, beside_half):
    half = rows // 2
    beside_last = y_swap(low(own(rows + half, 2 * rows) + wide(beside_half)))
    above_first = odd_swap(low(own(2 * rows, 2 * rows + half) + wide(above_half)))
    return beside_last, above_first


def add_halves(value, beside, above):
    half = value.shape[0] // 2
    return jnp.concatenate(
        [
            value[part * half : (part + 1) * half] + wide(beside[part]) + wide(above[part])
            for part in range(2)
        ],
        0,
    )


def share_two(value):
    return jnp.concatenate([value, y_swap(value)], 1)


def sum_two(value):
    rows = value.shape[1] // 2
    return value[:, :rows] + wide(y_swap(low(value[:, rows:])))


def on_device(
    tokens,
    side_input,
    prefix,
    positions,
    cotangent,
    query_weight,
    key_matrix,
    value_matrix,
    out_weight,
    gate_weight,
    up_weight,
    down_weight,
    laurel_left,
    laurel_right,
    side_gate_weight,
    side_out_weight,
    input_gain,
    laurel_gain,
    attention_gain,
    hidden_in_gain,
    hidden_out_gain,
    side_gain,
    query_gain,
    key_gain,
):
    shard_rows = query_weight.shape[0]
    place = Place(shard_rows)
    chips, depth = place.chips, place.depth
    sequences, own_rows, width = tokens.shape
    shape = tokens.shape
    side_width = side_input.shape[2]
    rank = laurel_left.shape[1]
    block_rows = positions.shape[1]
    query_width = query_weight.shape[1]
    key_width = key_matrix.shape[1]
    hidden_part = gate_weight.shape[1] // 4
    local_heads = query_width // HEAD_SIZE
    local_groups = key_width // HEAD_SIZE
    per_group = local_heads // local_groups

    near_rows = place.y * own_rows + jnp.arange(own_rows, dtype=jnp.int32)
    far_rows = (1 - place.y) * own_rows + jnp.arange(own_rows, dtype=jnp.int32)
    block_index = jnp.concatenate([near_rows, far_rows])
    row_index = place.z * block_rows + block_index
    near_positions = lax.dynamic_slice_in_dim(positions, place.y * own_rows, own_rows, 1)
    far_positions = lax.dynamic_slice_in_dim(positions, (1 - place.y) * own_rows, own_rows, 1)
    positions = jnp.concatenate([near_positions, far_positions], 1)
    freq = THETA ** (
        -(jnp.arange(HEAD_SIZE // 2, dtype=jnp.float32) * 2.0) / HEAD_SIZE
    )
    angle = positions.astype(jnp.float32)[..., None] * freq
    cosine = jnp.cos(angle)[..., None, :]
    sine = jnp.sin(angle)[..., None, :]

    inputs = tokens.astype(jnp.float32)
    normed, input_pull = jax.vjp(scaled_norm, inputs, input_gain)
    normed_reduced = normed.astype(jnp.bfloat16)
    flat_normed = normed_reduced.reshape(-1, width)
    half_width = width // 2
    everywhere = ("x", "core", "pair", "odd", "tp")

    small = jnp.concatenate(
        [laurel_left, laurel_right.T, side_gate_weight, side_out_weight.T], 1
    )
    small_full = lax.all_gather(small, everywhere, axis=0, tiled=True)
    out_shard, small_full = tie(out_weight.T, small_full)
    out_full = lax.all_gather(out_shard, everywhere[:4], axis=0, tiled=True)
    laurel_down = small_full[:, :rank]
    laurel_up_t = small_full[:, rank : 2 * rank]
    side_gate_full = small_full[:, 2 * rank : 2 * rank + side_width]
    side_out_t = small_full[:, 2 * rank + side_width :]

    mixed_shard = jnp.concatenate([query_weight, key_matrix, value_matrix], 1)
    gate_up = quarters(place, [gate_weight, up_weight])
    gate_up_arrived = odd_swap(take(gate_up, 1 - place.odd, 2))
    down = quarters(place, [down_weight.T])
    down_arrived = core_swap(take(down, 1 - place.core, 1))
    mixed_ring = [mixed_shard, z_shift(mixed_shard)]
    mixed_columns = [x_ring(place, mixed_shard)]
    down = in_order(place.core, take(down, place.core, 1), down_arrived, 0)
    down_kept, down_sent = take(down, place.odd, 2), take(down, 1 - place.odd, 2)
    near_in = place.move(flat_normed, place.whole_to_near).reshape(shape)
    near_in, mixed_ring[-1] = tie(near_in, mixed_ring[-1])
    flat_in = share_two(near_in)
    for step in range(2, depth):
        mixed_ring.append(z_shift(mixed_ring[-1]))
        mixed_columns.append(x_ring(place, mixed_ring[-2]))
        mixed_ring[-1], mixed_columns[-2] = tie(mixed_ring[-1], mixed_columns[-2])
        if step == 2:
            mixed_ring[-1], gate_up_arrived, down_kept, down_sent = tie(
                mixed_ring[-1], gate_up_arrived, down_kept, down_sent
            )
            down_arrived = odd_swap(down_sent)
    gate_up = in_order(place.odd, take(gate_up, place.odd, 2), gate_up_arrived, 0)
    gate_up_kept = take(gate_up, place.core, 2)
    gate_up_arrived = core_swap(take(gate_up, 1 - place.core, 2))
    mixed_ring[-1], mixed_columns[-1], flat_in, gate_up_arrived = tie(
        mixed_ring[-1], mixed_columns[-1], flat_in, gate_up_arrived
    )
    flat_in = flat_in.reshape(-1, width)
    mixed_columns.append(x_ring(place, mixed_ring[-1]))
    gate_up_shard = in_order(place.core, gate_up_kept, gate_up_arrived, 0).reshape(
        4 * shard_rows, -1
    )

    mixed_near = rows_of(place, mixed_columns)
    mixed_near, gate_up_shard, down_arrived = tie(mixed_near, gate_up_shard, down_arrived)
    mixed_far = core_swap(mixed_near)
    gate_up_shard, out_full = tie(gate_up_shard, out_full)
    gate_up_full = lax.all_gather(gate_up_shard, ("x", "pair"), axis=0, tiled=True)
    down_shard = in_order(place.odd, down_kept, down_arrived, 1).reshape(4 * shard_rows, -1)
    down_shard, gate_up_full = tie(down_shard, gate_up_full)
    down_full_t = lax.all_gather(down_shard, ("x", "pair"), axis=0, tiled=True)
    def project(first, last):
        return matmul(flat_in[:, :half_width], mixed_near[:, first:last]) + matmul(
            flat_in[:, half_width:], mixed_far[:, first:last]
        )

    key_value_raw = project(query_width, query_width + 2 * key_width)
    query_raw = project(0, query_width)

    def queries_of(part, gain):
        part = part.reshape(sequences, block_rows, local_heads, HEAD_SIZE)
        return rotate(scaled_norm(part, gain), cosine, sine)

    def keys_of(part, gain):
        keys = part[:, :key_width].reshape(sequences, block_rows, local_groups, HEAD_SIZE)
        values = part[:, key_width:].reshape(sequences, block_rows, local_groups, HEAD_SIZE)
        return rotate(scaled_norm(keys, gain), cosine, sine), plain_norm(values)

    (keys, values), keys_pull = jax.vjp(keys_of, key_value_raw, key_gain)
    query_rows, queries_pull = jax.vjp(queries_of, query_raw, query_gain)
    query_low = query_rows.astype(jnp.bfloat16).reshape(
        sequences, block_rows, local_groups, per_group, HEAD_SIZE
    )
    both = jnp.concatenate([low(keys), low(values)], 2)
    pieces = z_ring(place, both)
    key_index = jnp.concatenate(
        [((place.z - dz) % depth) * block_rows + block_index for dz in range(depth)]
    )
    everyone = jnp.concatenate(pieces, 1)
    all_keys = everyone[:, :, :local_groups]
    all_values = everyone[:, :, local_groups:]
    visible = (key_index[None, None, :] <= row_index[None, :, None]) | (
        key_index[None, None, :] < prefix[:, None, None]
    )

    def all_scores():
        scores = jnp.einsum(
            "sbkgd,sjkd->skgbj", query_low, all_keys, preferred_element_type=jnp.float32
        )
        return jnp.where(visible[:, None, None], scores, MASKED)

    scores = all_scores()
    highest = jnp.max(scores, axis=-1, keepdims=True)
    log_total = highest + jnp.log(jnp.sum(jnp.exp(scores - highest), axis=-1, keepdims=True))
    probs = jnp.exp(scores - log_total)
    probs_low = low(probs)
    attended = jnp.einsum(
        "skgbj,sjkd->sbkgd", probs_low, all_values, preferred_element_type=jnp.float32
    )
    attended_low = attended.astype(jnp.bfloat16).reshape(
        sequences * block_rows, local_heads * HEAD_SIZE
    )
    attention = sum_two(matmul_t(attended_low, out_full).reshape(sequences, block_rows, width))
    laurel_mid = matmul(flat_normed, laurel_down).astype(jnp.bfloat16)
    laurel_out = matmul_t(laurel_mid, laurel_up_t).reshape(shape)
    mixed, mix_pull = jax.vjp(
        attention_mix, inputs, attention, normed, laurel_out, attention_gain, laurel_gain
    )
    hidden_in, pre_pull = jax.vjp(scaled_norm, mixed, hidden_in_gain)
    hidden_block = share_four(
        to_fixed(place, low(hidden_in).reshape(-1, width))
    )

    hidden_block = add_core(hidden_block)
    gate_up_out = matmul(hidden_block, gate_up_full)
    hidden, hidden_pull = jax.vjp(
        geglu, gate_up_out[:, :hidden_part], gate_up_out[:, hidden_part:]
    )
    hidden_low = low(hidden)
    token_rows = sequences * own_rows

    def down_product(value):
        return matmul_t(value, down_full_t)

    far_out = low(down_product(hidden_low[4 * token_rows :]))
    own, _, above_half, beside_half, beside_first, above_last = sum_across(
        hidden_low, core_swap(far_out), down_product
    )
    beside_last, above_first = sum_beside(token_rows, own, above_half, beside_half)
    hidden_out = add_halves(
        own(0, token_rows), (beside_first, beside_last), (above_first, above_last)
    )
    hidden_out = from_fixed(place, hidden_out).reshape(shape)
    layer_out, post_pull = jax.vjp(residual_mix, mixed, hidden_out, hidden_out_gain)
    layer_low = layer_out.astype(jnp.bfloat16).reshape(-1, width)
    side_pre = matmul(layer_low, side_gate_full)
    side_act, side_pull = jax.vjp(
        geglu, side_pre, side_input.astype(jnp.float32).reshape(-1, side_width)
    )
    side_low = side_act.astype(jnp.bfloat16)
    projected = matmul_t(side_low, side_out_t).reshape(shape)
    result, final_pull = jax.vjp(residual_mix, layer_out, projected, side_gain)
    result = low(result)
    out_grad_first, projected_grad, side_gain_grad = final_pull(cotangent.astype(jnp.float32))
    projected_low = projected_grad.astype(jnp.bfloat16).reshape(-1, width)
    side_out_grad_t = matmul(projected_low.T, side_low)
    side_grad = matmul(projected_low, side_out_t)
    side_pre_grad, side_input_grad = side_pull(side_grad)
    side_pre_low = side_pre_grad.astype(jnp.bfloat16)
    side_gate_grad = matmul(layer_low.T, side_pre_low)
    layer_grad = out_grad_first + matmul_t(side_pre_low, side_gate_full).reshape(shape)
    mixed_grad_first, hidden_out_grad, hidden_out_gain_grad = post_pull(layer_grad)
    hidden_out_block = add_core(
        share_four(to_fixed(place, low(hidden_out_grad).reshape(-1, width)))
    )

    side_grads = lax.psum_scatter(
        low(jnp.concatenate([side_gate_grad, side_out_grad_t], 1)),
        everywhere[:4],
        scatter_dimension=0,
        tiled=True,
    )
    down_grad = low(matmul(hidden_out_block.T, hidden_low))
    hidden_out_block, down_grad = tie(hidden_out_block, down_grad)
    down_grad, side_grads = tie(down_grad, side_grads)
    down_grad = lax.psum_scatter(down_grad, ("x", "pair"), scatter_dimension=0, tiled=True)
    hidden_grad = matmul(hidden_out_block, down_full_t)
    gate_grad_full, up_grad_full = hidden_pull(hidden_grad)
    gate_up_low = jnp.concatenate([low(gate_grad_full), low(up_grad_full)], 1)

    def gate_up_product(value):
        return matmul_t(value, gate_up_full)

    far_out = low(gate_up_product(gate_up_low[4 * token_rows :]))
    own, across, above_half, beside_half, beside_first, above_last = sum_across(
        gate_up_low, core_swap(far_out), gate_up_product
    )
    wgrad_low, across = tie(gate_up_low, across)
    gate_up_grad = low(matmul(hidden_block.T, wgrad_low))
    beside_last, above_first = sum_beside(token_rows, own, above_half, beside_half)
    hidden_in_sum = own(0, token_rows)
    hidden_in_sum, gate_up_grad = tie(hidden_in_sum, gate_up_grad)
    hidden_in_sum = add_halves(
        hidden_in_sum, (beside_first, beside_last), (above_first, above_last)
    )
    hidden_in_sum = from_fixed(place, hidden_in_sum).reshape(shape)
    gate_up_grad = lax.psum_scatter(
        gate_up_grad, ("x", "pair"), scatter_dimension=0, tiled=True
    )
    mixed_grad_second, hidden_in_gain_grad = pre_pull(hidden_in_sum)
    mixed_grad = mixed_grad_first + mixed_grad_second
    (
        inputs_grad_first,
        attention_grad,
        normed_grad_first,
        laurel_grad,
        attention_gain_grad,
        laurel_gain_grad,
    ) = mix_pull(mixed_grad)
    attention_grad, down_grad = tie(attention_grad, down_grad)
    attention_block = share_two(low(attention_grad)).reshape(-1, width)
    (down_grad_t,) = join_four(place, wide(down_grad), 1)

    attended_grad = (
        matmul(attention_block, out_full)
        .astype(jnp.bfloat16)
        .reshape(sequences, block_rows, local_groups, per_group, HEAD_SIZE)
    )
    laurel_low = laurel_grad.astype(jnp.bfloat16).reshape(-1, width)
    laurel_mid_grad = matmul(laurel_low, laurel_up_t).astype(jnp.bfloat16)
    normed_grad_second = matmul_t(laurel_mid_grad, laurel_down).reshape(shape)

    def scatter_attention(left, right, extra=None):
        def rows(start, end):
            value = matmul(left[:, start:end].T, right)
            return value if extra is None else jnp.concatenate([value, extra[start:end]], 1)

        arrived = core_swap(low(rows(half_width, width)))

        def partial(dx, first, last):
            start, end = (dx * depth + first) * shard_rows, (dx * depth + last) * shard_rows
            return rows(start, end) + wide(arrived[start:end])

        return scatter_x(place, partial, [(1, depth), (0, 1)])

    near_own = near_in.reshape(-1, width)
    laurel_near = place.move(laurel_low, place.whole_to_near)
    out_parts = scatter_attention(
        place.move(attention_block, place.whole_to_near),
        attended_low,
        jnp.concatenate(
            [matmul(near_own.T, laurel_mid_grad), matmul(laurel_near.T, laurel_mid)], 1
        ),
    )

    delta = jnp.transpose(
        jnp.sum(attended_grad.astype(jnp.float32) * attended, axis=-1), (0, 2, 3, 1)
    )
    probs = jnp.exp(all_scores() - log_total)
    probs_grad = jnp.einsum(
        "sbkgd,sjkd->skgbj", attended_grad, all_values, preferred_element_type=jnp.float32
    )
    scores_grad = low(probs * (probs_grad - delta[..., None]))
    query_grad = jnp.einsum(
        "skgbj,sjkd->sbkgd", scores_grad, all_keys, preferred_element_type=jnp.float32
    )
    keys_grad = jnp.einsum(
        "skgbj,sbkgd->sjkd", scores_grad, query_low, preferred_element_type=jnp.float32
    )
    values_grad = jnp.einsum(
        "skgbj,sbkgd->sjkd", low(probs), attended_grad, preferred_element_type=jnp.float32
    )
    both_grad = jnp.concatenate([keys_grad, values_grad], 2)
    passing = None
    for step in range(1, depth + 1):
        dz = step % depth
        value = both_grad[:, dz * block_rows : (dz + 1) * block_rows]
        if passing is not None:
            value = value + wide(passing)
        if dz:
            passing = z_shift(low(value))
    value, gate_up_grad = tie(value, gate_up_grad)
    out_parts, value = tie(out_parts, value)
    out_sum = scatter_z(place, out_parts)
    query_raw_grad, query_gain_grad = queries_pull(
        query_grad.reshape(sequences, block_rows, local_heads, HEAD_SIZE)
    )
    keys_raw_grad, key_gain_grad = keys_pull(
        (value[:, :, :local_groups], value[:, :, local_groups:])
    )
    mixed_low = jnp.concatenate([low(query_raw_grad), low(keys_raw_grad)], 1)
    mixed_weight_grad = scatter_z(place, scatter_attention(flat_in, mixed_low))
    block_in_grad = jnp.concatenate(
        [matmul_t(mixed_low, mixed_near), matmul_t(mixed_low, mixed_far)], 1
    ).reshape(sequences, block_rows, width)
    block_in_sum = place.move(
        sum_two(block_in_grad).reshape(-1, width), place.near_to_whole
    ).reshape(shape)
    normed_grad = normed_grad_first + normed_grad_second + block_in_sum
    inputs_grad_second, input_gain_grad = input_pull(normed_grad)
    tokens_grad = inputs_grad_first + inputs_grad_second
    gain_grads = (
        jnp.stack(
            [
                input_gain_grad,
                laurel_gain_grad,
                attention_gain_grad,
                hidden_in_gain_grad,
                hidden_out_gain_grad,
                side_gain_grad,
            ]
        )
    )
    head_grads = jnp.concatenate(
        [query_gain_grad, key_gain_grad, jnp.zeros((width - 2 * HEAD_SIZE,), jnp.float32)]
    )
    gain_grads = sum_everywhere(place, jnp.concatenate([gain_grads, head_grads[None]], 0))
    gain_grads = tuple(gain_grads[:6]) + (
        gain_grads[6, :HEAD_SIZE],
        gain_grads[6, HEAD_SIZE : 2 * HEAD_SIZE],
    )
    gate_grad, up_grad = join_four(place, wide(gate_up_grad), 2)
    kept, sent = halves_of(
        jnp.concatenate([out_sum[:, query_width:], wide(side_grads)], 1), 0, place.y
    )
    small_grads = kept + wide(y_swap(low(sent)))
    side_input_grad = side_input_grad.reshape(sequences, own_rows, side_width)
    return (
        (result, tokens_grad, side_input_grad)
        + (
            mixed_weight_grad[:, :query_width],
            mixed_weight_grad[:, query_width : query_width + key_width],
            mixed_weight_grad[:, query_width + key_width :],
            out_sum[:, :query_width].T,
            gate_grad,
            up_grad,
            down_grad_t.T,
        )
        + (
            small_grads[:, :rank],
            small_grads[:, rank : 2 * rank].T,
            small_grads[:, 2 * rank : 2 * rank + side_width],
            small_grads[:, 2 * rank + side_width :].T,
        )
        + gain_grads
    )


def solution(mesh):
    sizes = (mesh.shape["fsdp"] // 2, 2, mesh.shape["ctx"] // 2, 2, mesh.shape["tp"])
    mesh = Mesh(mesh.devices.reshape(sizes), ("x", "core", "pair", "odd", "tp"))
    placed = (
        P(("x", "core"), ("pair", "odd", "tp"), None),
        P(("x", "core"), ("pair", "odd", "tp"), None),
        P(("x", "core")),
        P(("x", "core"), ("pair", "odd")),
        P(("x", "core"), ("pair", "odd", "tp"), None),
        P(("x", "core", "pair", "odd"), "tp"),
        P(("x", "core", "pair", "odd"), "tp"),
        P(("x", "core", "pair", "odd"), "tp"),
        P("tp", ("x", "core", "pair", "odd")),
        P(("x", "core", "pair", "odd"), "tp"),
        P(("x", "core", "pair", "odd"), "tp"),
        P("tp", ("x", "core", "pair", "odd")),
        P(("x", "core", "pair", "odd", "tp"), None),
        P(None, ("x", "core", "pair", "odd", "tp")),
        P(("x", "core", "pair", "odd", "tp"), None),
        P(None, ("x", "core", "pair", "odd", "tp")),
        P(),
        P(),
        P(),
        P(),
        P(),
        P(),
        P(),
        P(),
    )
    return jax.shard_map(
        on_device,
        mesh=mesh,
        in_specs=placed,
        out_specs=(
            P(("x", "core"), ("pair", "odd", "tp"), None),
            P(("x", "core"), ("pair", "odd", "tp"), None),
            P(("x", "core"), ("pair", "odd", "tp"), None),
            P(("x", "core", "pair", "odd"), "tp"),
            P(("x", "core", "pair", "odd"), "tp"),
            P(("x", "core", "pair", "odd"), "tp"),
            P("tp", ("x", "core", "pair", "odd")),
            P(("x", "core", "pair", "odd"), "tp"),
            P(("x", "core", "pair", "odd"), "tp"),
            P("tp", ("x", "core", "pair", "odd")),
            P(("x", "core", "pair", "odd", "tp"), None),
            P(None, ("x", "core", "pair", "odd", "tp")),
            P(("x", "core", "pair", "odd", "tp"), None),
            P(None, ("x", "core", "pair", "odd", "tp")),
            P(),
            P(),
            P(),
            P(),
            P(),
            P(),
            P(),
            P(),
        ),
        check_vma=False,
    )
```

```python
import jax
import jax.numpy as jnp
from jax import lax
from jax.experimental import pallas as pl
from jax.experimental.pallas import tpu as pltpu
from jax.sharding import Mesh, PartitionSpec as P

HEAD_SIZE = 256


EPS = 1e-06
THETA = 1000000.0
MASKED = -1e30
SQRT_HALF = 0.7071067811865476
LANES = 128


def scaled_norm(value, gain):
    return value * lax.rsqrt(jnp.mean(value * value, axis=-1, keepdims=True) + EPS) * gain


def plain_norm(value):
    return value * lax.rsqrt(jnp.mean(value * value, axis=-1, keepdims=True) + EPS)


def rotate(value, cosine, sine):
    half = value.shape[-1] // 2
    first = value[..., :half]
    second = value[..., half:]
    return jnp.concatenate(
        [first * cosine - second * sine, second * cosine + first * sine], axis=-1
    )


def geglu(gate, upward):
    return jax.nn.gelu(gate, approximate=True) * upward


def attention_mix(inputs, attention, normed, laurel, attention_gain, laurel_gain):
    return (
        inputs + scaled_norm(attention, attention_gain) + normed + scaled_norm(laurel, laurel_gain)
    ) * SQRT_HALF


def residual_mix(residual, branch, gain):
    return residual + scaled_norm(branch, gain)


def matmul(left, right):
    return jnp.dot(left, right, preferred_element_type=jnp.float32)


def matmul_t(left, right):
    return lax.dot_general(
        left, right, (((1,), (1,)), ((), ())), preferred_element_type=jnp.float32
    )


def low(value):
    return value.astype(jnp.bfloat16)


def wide(value):
    return value.astype(jnp.float32)


def tie(*values):
    return lax.optimization_barrier(values)


CTX = ("pair", "odd")


def core_swap(value):
    return lax.ppermute(value, "core", [(0, 1), (1, 0)])


def x_shift(value, step=1):
    size = lax.axis_size("x")
    return lax.ppermute(value, "x", [(i, (i + step) % size) for i in range(size)])


def z_shift(value, step=1):
    size = lax.axis_size(CTX)
    return lax.ppermute(value, CTX, [(i, (i + step) % size) for i in range(size)])


def pair_shift(value):
    size = lax.axis_size("pair")
    return lax.ppermute(value, "pair", [(i, (i + 1) % size) for i in range(size)])


def odd_swap(value):
    return lax.ppermute(value, "odd", [(0, 1), (1, 0)])


def y_swap(value):
    return lax.ppermute(value, "tp", [(0, 1), (1, 0)])


def in_order(own, mine, other, axis):
    first = jnp.where(own == 0, mine, other)
    second = jnp.where(own == 0, other, mine)
    return jnp.stack([first, second], axis)


def halves_of(value, axis, own):
    shape = value.shape
    value = value.reshape(shape[:axis] + (2, shape[axis] // 2) + shape[axis + 1 :])
    kept = lax.dynamic_index_in_dim(value, own, axis, False)
    return kept, lax.dynamic_index_in_dim(value, 1 - own, axis, False)


class Place:
    def __init__(self, rows):
        self.rows = rows
        self.chips = chips = lax.axis_size("x")
        self.pairs = pairs = lax.axis_size("pair")
        self.depth = depth = 2 * pairs
        self.core = core = lax.axis_index("core")
        self.x = x = lax.axis_index("x")
        self.y = lax.axis_index("tp")
        self.pair = pair = lax.axis_index("pair")
        self.odd = lax.axis_index("odd")
        self.z = z = pair * 2 + self.odd
        count = 2 * chips * depth

        def whole(xs, cores, zs):
            return (xs * 2 + cores) * depth + zs

        def near(xs, cores, zs):
            return (((core + cores) % 2) * chips + (x - xs) % chips) * depth + (z - zs) % depth

        at = jnp.arange(count, dtype=jnp.int32)
        of_whole = (at // (2 * depth), (at // depth) % 2, at % depth)
        of_near = (
            (x - (at // depth) % chips) % chips,
            (core + at // (chips * depth)) % 2,
            (z - at) % depth,
        )
        self.whole_to_near = whole(*of_near).astype(jnp.int32)
        self.near_to_whole = near(*of_whole).astype(jnp.int32)

    def move(self, value, index):
        rows = self.rows
        if rows % LANES:
            shape = value.shape
            value = value.reshape(shape[0], -1, rows)
            return jnp.take(value, index, axis=1).reshape(shape)

        def kernel(index_ref, value_ref, out_ref):
            for i in range(value.shape[1] // rows):
                start = pl.multiple_of(index_ref[i] * rows, LANES)
                out_ref[:, i * rows : (i + 1) * rows] = value_ref[:, pl.ds(start, rows)]

        return pl.pallas_call(
            kernel,
            out_shape=jax.ShapeDtypeStruct(value.shape, value.dtype),
            in_specs=[
                pl.BlockSpec(memory_space=pltpu.SMEM),
                pl.BlockSpec(memory_space=pltpu.VMEM),
            ],
            out_specs=pl.BlockSpec(memory_space=pltpu.VMEM),
            name="move_blocks",
        )(index, value)


def z_ring(place, shard):
    ring = [shard]
    for _ in range(1, place.depth):
        ring.append(z_shift(ring[-1]))
    return ring


def rows_of(place, columns):
    return jnp.concatenate(
        [column[dx] for dx in range(place.chips) for column in columns], 0
    )


def scatter_x(place, partial, splits):
    rows = place.rows
    parts = {}
    for first, last in splits:
        run = None
        for dx in range(1, place.chips):
            value = partial(dx, first, last)
            if run is not None:
                value = value + wide(run)
            run = x_shift(low(value))
        value = partial(0, first, last)
        if run is not None:
            value = value + wide(run)
        for dz in range(first, last):
            parts[dz] = value[(dz - first) * rows : (dz - first + 1) * rows]
    return parts


def scatter_z(place, parts):
    passing = None
    for step in range(1, place.depth):
        value = parts[step]
        if passing is not None:
            value = value + wide(passing)
        passing = z_shift(low(value))
    return parts[0] + wide(passing)


def sum_everywhere(place, value):
    value = value + core_swap(value)
    value = value + y_swap(value)
    value = sum([x_shift(value, step) for step in range(1, place.chips)], value)
    return sum([z_shift(value, step) for step in range(1, place.depth)], value)


def swap_middle(place, value, first):
    second = 2 * place.pairs // first
    size = 2 * place.rows
    return jnp.concatenate(
        [
            value[:, ((x * first + a) * second + b) * size :][:, :size]
            for x in range(place.chips)
            for b in range(second)
            for a in range(first)
        ],
        1,
    )


def to_fixed(place, value):
    return swap_middle(place, value, 2)


def from_fixed(place, value):
    return swap_middle(place, value, place.pairs)


def take(value, index, axis):
    return lax.dynamic_index_in_dim(value, index, axis, False)


def quarters(place, shards):
    return jnp.concatenate([shard.reshape(place.rows, 2, 2, -1) for shard in shards], 3)


def join_four(place, value, parts):
    rows = place.rows
    value = value.reshape(2, 2, rows, -1)
    kept = lax.dynamic_index_in_dim(value, place.odd, 1, False)
    sent = lax.dynamic_index_in_dim(value, 1 - place.odd, 1, False)
    value = in_order(place.odd, kept, wide(odd_swap(low(sent))), 2)
    kept = lax.dynamic_index_in_dim(value, place.core, 0, False)
    sent = lax.dynamic_index_in_dim(value, 1 - place.core, 0, False)
    value = in_order(place.core, kept, core_swap(sent), 1)
    return [part.reshape(rows, -1) for part in jnp.split(value, parts, 3)]


def x_ring(place, piece):
    pieces = [piece]
    for _ in range(1, place.chips):
        pieces.append(x_shift(pieces[-1]))
    return pieces


def share_four(value):
    half = value.shape[0] // 2
    beside = y_swap(value)
    above = odd_swap(value)
    across = [y_swap(above[:half]), odd_swap(beside[half:])]
    return jnp.concatenate([value, beside, above] + across, 0)


def add_core(value):
    return jnp.concatenate([value, core_swap(value)], 0)


def sum_across(value, arrived, product):
    rows = value.shape[0] // 8
    half = rows // 2

    def own(first, last):
        return product(value[first:last]) + wide(arrived[first:last])

    across = low(own(3 * rows, 4 * rows))
    above_half = y_swap(across[:half])
    beside_half = odd_swap(across[half:])
    beside_first = y_swap(low(own(rows, rows + half)))
    above_last = odd_swap(low(own(2 * rows + half, 3 * rows)))
    return own, across, above_half, beside_half, beside_first, above_last


def sum_beside(rows, own, above_half, beside_half):
    half = rows // 2
    beside_last = y_swap(low(own(rows + half, 2 * rows) + wide(beside_half)))
    above_first = odd_swap(low(own(2 * rows, 2 * rows + half) + wide(above_half)))
    return beside_last, above_first


def add_halves(value, beside, above):
    half = value.shape[0] // 2
    return jnp.concatenate(
        [
            value[part * half : (part + 1) * half] + wide(beside[part]) + wide(above[part])
            for part in range(2)
        ],
        0,
    )


def share_two(value):
    return jnp.concatenate([value, y_swap(value)], 1)


def sum_two(value):
    rows = value.shape[1] // 2
    return value[:, :rows] + wide(y_swap(low(value[:, rows:])))


GELU_SCALE = 0.7978845608028654
GELU_CUBE = 0.044715


def gelu_parts(gate):
    square = gate * gate
    bend = jnp.tanh(GELU_SCALE * gate * (1.0 + GELU_CUBE * square))
    half = 0.5 + 0.5 * bend
    slope = half + 0.5 * gate * (1.0 - bend * bend) * (
        GELU_SCALE * (1.0 + 3.0 * GELU_CUBE * square)
    )
    return gate * half, slope


def hidden_backward(block, weights, both):
    rows, width = block.shape
    units = weights.shape[1]
    tile, chunk = min(512, rows), min(256, units)

    def kernel(block_ref, weights_ref, both_ref, out_ref):
        for start in range(0, units, chunk):
            grad = jnp.dot(
                block_ref[...],
                weights_ref[:, start : start + chunk],
                preferred_element_type=jnp.float32,
            )
            value, slope = gelu_parts(both_ref[:, start : start + chunk])
            up = both_ref[:, units + start : units + start + chunk]
            out_ref[:, start : start + chunk] = (grad * up * slope).astype(jnp.bfloat16)
            out_ref[:, units + start : units + start + chunk] = (grad * value).astype(
                jnp.bfloat16
            )

    return pl.pallas_call(
        kernel,
        grid=(rows // tile,),
        in_specs=[
            pl.BlockSpec((tile, width), lambda i: (i, 0)),
            pl.BlockSpec((width, units), lambda i: (0, 0)),
            pl.BlockSpec((tile, 2 * units), lambda i: (i, 0)),
        ],
        out_specs=pl.BlockSpec((tile, 2 * units), lambda i: (i, 0)),
        out_shape=jax.ShapeDtypeStruct((rows, 2 * units), jnp.bfloat16),
        compiler_params=pltpu.CompilerParams(vmem_limit_bytes=56 * 2**20),
        cost_estimate=pl.CostEstimate(
            flops=2 * rows * width * units,
            transcendentals=rows * units,
            bytes_accessed=2 * rows * width + 2 * width * units + 12 * rows * units,
        ),
        name="hidden_backward",
    )(block, weights, both)


def on_device(
    tokens,
    side_input,
    prefix,
    positions,
    cotangent,
    query_weight,
    key_matrix,
    value_matrix,
    out_weight,
    gate_weight,
    up_weight,
    down_weight,
    laurel_left,
    laurel_right,
    side_gate_weight,
    side_out_weight,
    input_gain,
    laurel_gain,
    attention_gain,
    hidden_in_gain,
    hidden_out_gain,
    side_gain,
    query_gain,
    key_gain,
):
    shard_rows = query_weight.shape[0]
    place = Place(shard_rows)
    chips, depth = place.chips, place.depth
    sequences, own_rows, width = tokens.shape
    shape = tokens.shape
    side_width = side_input.shape[2]
    rank = laurel_left.shape[1]
    block_rows = positions.shape[1]
    query_width = query_weight.shape[1]
    key_width = key_matrix.shape[1]
    hidden_part = gate_weight.shape[1] // 4
    local_heads = query_width // HEAD_SIZE
    local_groups = key_width // HEAD_SIZE
    per_group = local_heads // local_groups

    near_rows = place.y * own_rows + jnp.arange(own_rows, dtype=jnp.int32)
    far_rows = (1 - place.y) * own_rows + jnp.arange(own_rows, dtype=jnp.int32)
    block_index = jnp.concatenate([near_rows, far_rows])
    row_index = place.z * block_rows + block_index
    near_positions = lax.dynamic_slice_in_dim(positions, place.y * own_rows, own_rows, 1)
    far_positions = lax.dynamic_slice_in_dim(positions, (1 - place.y) * own_rows, own_rows, 1)
    positions = jnp.concatenate([near_positions, far_positions], 1)
    freq = THETA ** (
        -(jnp.arange(HEAD_SIZE // 2, dtype=jnp.float32) * 2.0) / HEAD_SIZE
    )
    angle = positions.astype(jnp.float32)[..., None] * freq
    cosine = jnp.cos(angle)[..., None, :]
    sine = jnp.sin(angle)[..., None, :]

    inputs = tokens.astype(jnp.float32)
    normed, input_pull = jax.vjp(scaled_norm, inputs, input_gain)
    normed_reduced = normed.astype(jnp.bfloat16)
    flat_normed = normed_reduced.reshape(-1, width)
    half_width = width // 2
    everywhere = ("x", "core", "pair", "odd", "tp")

    small = jnp.concatenate(
        [laurel_left, laurel_right.T, side_gate_weight, side_out_weight.T], 1
    )
    small_full = lax.all_gather(small, everywhere, axis=0, tiled=True)
    out_shard, small_full = tie(out_weight.T, small_full)
    out_full = lax.all_gather(out_shard, everywhere[:4], axis=0, tiled=True)
    laurel_down = small_full[:, :rank]
    laurel_up_t = small_full[:, rank : 2 * rank]
    side_gate_full = small_full[:, 2 * rank : 2 * rank + side_width]
    side_out_t = small_full[:, 2 * rank + side_width :]

    mixed_shard = jnp.concatenate([query_weight, key_matrix, value_matrix], 1)
    gate_up = quarters(place, [gate_weight, up_weight])
    gate_up_arrived = odd_swap(take(gate_up, 1 - place.odd, 2))
    down = quarters(place, [down_weight.T])
    down_arrived = core_swap(take(down, 1 - place.core, 1))
    mixed_ring = [mixed_shard, z_shift(mixed_shard)]
    mixed_columns = [x_ring(place, mixed_shard)]
    down = in_order(place.core, take(down, place.core, 1), down_arrived, 0)
    down_kept, down_sent = take(down, place.odd, 2), take(down, 1 - place.odd, 2)
    near_in = place.move(flat_normed, place.whole_to_near).reshape(shape)
    near_in, mixed_ring[-1] = tie(near_in, mixed_ring[-1])
    flat_in = share_two(near_in)
    for step in range(2, depth):
        mixed_ring.append(z_shift(mixed_ring[-1]))
        mixed_columns.append(x_ring(place, mixed_ring[-2]))
        mixed_ring[-1], mixed_columns[-2] = tie(mixed_ring[-1], mixed_columns[-2])
        if step == 2:
            mixed_ring[-1], gate_up_arrived, down_kept, down_sent = tie(
                mixed_ring[-1], gate_up_arrived, down_kept, down_sent
            )
            down_arrived = odd_swap(down_sent)
    gate_up = in_order(place.odd, take(gate_up, place.odd, 2), gate_up_arrived, 0)
    gate_up_kept = take(gate_up, place.core, 2)
    gate_up_arrived = core_swap(take(gate_up, 1 - place.core, 2))
    mixed_ring[-1], mixed_columns[-1], flat_in, gate_up_arrived = tie(
        mixed_ring[-1], mixed_columns[-1], flat_in, gate_up_arrived
    )
    flat_in = flat_in.reshape(-1, width)
    mixed_columns.append(x_ring(place, mixed_ring[-1]))
    gate_up_shard = in_order(place.core, gate_up_kept, gate_up_arrived, 0).reshape(
        4 * shard_rows, -1
    )

    mixed_near = rows_of(place, mixed_columns)
    mixed_near, gate_up_shard, down_arrived = tie(mixed_near, gate_up_shard, down_arrived)
    mixed_far = core_swap(mixed_near)
    gate_up_shard, out_full = tie(gate_up_shard, out_full)
    gate_up_full = lax.all_gather(gate_up_shard, ("x", "pair"), axis=0, tiled=True)
    down_shard = in_order(place.odd, down_kept, down_arrived, 1).reshape(4 * shard_rows, -1)
    down_shard, gate_up_full = tie(down_shard, gate_up_full)
    down_full_t = lax.all_gather(down_shard, ("x", "pair"), axis=0, tiled=True)
    def project(first, last):
        return matmul(flat_in[:, :half_width], mixed_near[:, first:last]) + matmul(
            flat_in[:, half_width:], mixed_far[:, first:last]
        )

    key_value_raw = project(query_width, query_width + 2 * key_width)
    query_raw = project(0, query_width)

    def queries_of(part, gain):
        part = part.reshape(sequences, block_rows, local_heads, HEAD_SIZE)
        return rotate(scaled_norm(part, gain), cosine, sine)

    def keys_of(part, gain):
        keys = part[:, :key_width].reshape(sequences, block_rows, local_groups, HEAD_SIZE)
        values = part[:, key_width:].reshape(sequences, block_rows, local_groups, HEAD_SIZE)
        return rotate(scaled_norm(keys, gain), cosine, sine), plain_norm(values)

    (keys, values), keys_pull = jax.vjp(keys_of, key_value_raw, key_gain)
    query_rows, queries_pull = jax.vjp(queries_of, query_raw, query_gain)
    query_low = query_rows.astype(jnp.bfloat16).reshape(
        sequences, block_rows, local_groups, per_group, HEAD_SIZE
    )
    both = jnp.concatenate([low(keys), low(values)], 2)
    pieces = z_ring(place, both)
    key_index = jnp.concatenate(
        [((place.z - dz) % depth) * block_rows + block_index for dz in range(depth)]
    )
    everyone = jnp.concatenate(pieces, 1)
    all_keys = everyone[:, :, :local_groups]
    all_values = everyone[:, :, local_groups:]
    visible = (key_index[None, None, :] <= row_index[None, :, None]) | (
        key_index[None, None, :] < prefix[:, None, None]
    )

    def all_scores():
        scores = jnp.einsum(
            "sbkgd,sjkd->skgbj", query_low, all_keys, preferred_element_type=jnp.float32
        )
        return jnp.where(visible[:, None, None], scores, MASKED)

    scores = all_scores()
    highest = jnp.max(scores, axis=-1, keepdims=True)
    log_total = highest + jnp.log(jnp.sum(jnp.exp(scores - highest), axis=-1, keepdims=True))
    probs = jnp.exp(scores - log_total)
    probs_low = low(probs)
    attended = jnp.einsum(
        "skgbj,sjkd->sbkgd", probs_low, all_values, preferred_element_type=jnp.float32
    )
    attended_low = attended.astype(jnp.bfloat16).reshape(
        sequences * block_rows, local_heads * HEAD_SIZE
    )
    attention = sum_two(matmul_t(attended_low, out_full).reshape(sequences, block_rows, width))
    laurel_mid = matmul(flat_normed, laurel_down).astype(jnp.bfloat16)
    laurel_out = matmul_t(laurel_mid, laurel_up_t).reshape(shape)
    mixed, mix_pull = jax.vjp(
        attention_mix, inputs, attention, normed, laurel_out, attention_gain, laurel_gain
    )
    hidden_in, pre_pull = jax.vjp(scaled_norm, mixed, hidden_in_gain)
    hidden_block = share_four(
        to_fixed(place, low(hidden_in).reshape(-1, width))
    )

    hidden_block = add_core(hidden_block)
    gate_up_out = matmul(hidden_block, gate_up_full)
    hidden_low = low(geglu(gate_up_out[:, :hidden_part], gate_up_out[:, hidden_part:]))
    token_rows = sequences * own_rows

    def down_product(value):
        return matmul_t(value, down_full_t)

    far_out = low(down_product(hidden_low[4 * token_rows :]))
    own, _, above_half, beside_half, beside_first, above_last = sum_across(
        hidden_low, core_swap(far_out), down_product
    )
    beside_last, above_first = sum_beside(token_rows, own, above_half, beside_half)
    hidden_out = add_halves(
        own(0, token_rows), (beside_first, beside_last), (above_first, above_last)
    )
    hidden_out = from_fixed(place, hidden_out).reshape(shape)
    layer_out, post_pull = jax.vjp(residual_mix, mixed, hidden_out, hidden_out_gain)
    layer_low = layer_out.astype(jnp.bfloat16).reshape(-1, width)
    side_pre = matmul(layer_low, side_gate_full)
    side_act, side_pull = jax.vjp(
        geglu, side_pre, side_input.astype(jnp.float32).reshape(-1, side_width)
    )
    side_low = side_act.astype(jnp.bfloat16)
    projected = matmul_t(side_low, side_out_t).reshape(shape)
    result, final_pull = jax.vjp(residual_mix, layer_out, projected, side_gain)
    result = low(result)
    out_grad_first, projected_grad, side_gain_grad = final_pull(cotangent.astype(jnp.float32))
    projected_low = projected_grad.astype(jnp.bfloat16).reshape(-1, width)
    side_out_grad_t = matmul(projected_low.T, side_low)
    side_grad = matmul(projected_low, side_out_t)
    side_pre_grad, side_input_grad = side_pull(side_grad)
    side_pre_low = side_pre_grad.astype(jnp.bfloat16)
    side_gate_grad = matmul(layer_low.T, side_pre_low)
    layer_grad = out_grad_first + matmul_t(side_pre_low, side_gate_full).reshape(shape)
    mixed_grad_first, hidden_out_grad, hidden_out_gain_grad = post_pull(layer_grad)
    hidden_out_block = add_core(
        share_four(to_fixed(place, low(hidden_out_grad).reshape(-1, width)))
    )

    side_grads = lax.psum_scatter(
        low(jnp.concatenate([side_gate_grad, side_out_grad_t], 1)),
        everywhere[:4],
        scatter_dimension=0,
        tiled=True,
    )
    down_grad = low(matmul(hidden_out_block.T, hidden_low))
    hidden_out_block, down_grad = tie(hidden_out_block, down_grad)
    down_grad, side_grads = tie(down_grad, side_grads)
    down_grad = lax.psum_scatter(down_grad, ("x", "pair"), scatter_dimension=0, tiled=True)
    gate_up_low = hidden_backward(hidden_out_block, down_full_t, gate_up_out)

    def gate_up_product(value):
        return matmul_t(value, gate_up_full)

    far_out = low(gate_up_product(gate_up_low[4 * token_rows :]))
    own, across, above_half, beside_half, beside_first, above_last = sum_across(
        gate_up_low, core_swap(far_out), gate_up_product
    )
    wgrad_low, across = tie(gate_up_low, across)
    gate_up_grad = low(matmul(hidden_block.T, wgrad_low))
    beside_last, above_first = sum_beside(token_rows, own, above_half, beside_half)
    hidden_in_sum = own(0, token_rows)
    hidden_in_sum, gate_up_grad = tie(hidden_in_sum, gate_up_grad)
    hidden_in_sum = add_halves(
        hidden_in_sum, (beside_first, beside_last), (above_first, above_last)
    )
    hidden_in_sum = from_fixed(place, hidden_in_sum).reshape(shape)
    gate_up_grad = lax.psum_scatter(
        gate_up_grad, ("x", "pair"), scatter_dimension=0, tiled=True
    )
    mixed_grad_second, hidden_in_gain_grad = pre_pull(hidden_in_sum)
    mixed_grad = mixed_grad_first + mixed_grad_second
    (
        inputs_grad_first,
        attention_grad,
        normed_grad_first,
        laurel_grad,
        attention_gain_grad,
        laurel_gain_grad,
    ) = mix_pull(mixed_grad)
    attention_grad, down_grad = tie(attention_grad, down_grad)
    attention_block = share_two(low(attention_grad)).reshape(-1, width)
    (down_grad_t,) = join_four(place, wide(down_grad), 1)

    attended_grad = (
        matmul(attention_block, out_full)
        .astype(jnp.bfloat16)
        .reshape(sequences, block_rows, local_groups, per_group, HEAD_SIZE)
    )
    laurel_low = laurel_grad.astype(jnp.bfloat16).reshape(-1, width)
    laurel_mid_grad = matmul(laurel_low, laurel_up_t).astype(jnp.bfloat16)
    normed_grad_second = matmul_t(laurel_mid_grad, laurel_down).reshape(shape)

    def scatter_attention(left, right, extra=None):
        def rows(start, end):
            value = matmul(left[:, start:end].T, right)
            return value if extra is None else jnp.concatenate([value, extra[start:end]], 1)

        arrived = core_swap(low(rows(half_width, width)))

        def partial(dx, first, last):
            start, end = (dx * depth + first) * shard_rows, (dx * depth + last) * shard_rows
            return rows(start, end) + wide(arrived[start:end])

        return scatter_x(place, partial, [(1, depth), (0, 1)])

    near_own = near_in.reshape(-1, width)
    laurel_near = place.move(laurel_low, place.whole_to_near)
    out_parts = scatter_attention(
        place.move(attention_block, place.whole_to_near),
        attended_low,
        jnp.concatenate(
            [matmul(near_own.T, laurel_mid_grad), matmul(laurel_near.T, laurel_mid)], 1
        ),
    )

    delta = jnp.transpose(
        jnp.sum(attended_grad.astype(jnp.float32) * attended, axis=-1), (0, 2, 3, 1)
    )
    probs = jnp.exp(all_scores() - log_total)
    probs_grad = jnp.einsum(
        "sbkgd,sjkd->skgbj", attended_grad, all_values, preferred_element_type=jnp.float32
    )
    scores_grad = low(probs * (probs_grad - delta[..., None]))
    query_grad = jnp.einsum(
        "skgbj,sjkd->sbkgd", scores_grad, all_keys, preferred_element_type=jnp.float32
    )
    keys_grad = jnp.einsum(
        "skgbj,sbkgd->sjkd", scores_grad, query_low, preferred_element_type=jnp.float32
    )
    values_grad = jnp.einsum(
        "skgbj,sbkgd->sjkd", low(probs), attended_grad, preferred_element_type=jnp.float32
    )
    both_grad = jnp.concatenate([keys_grad, values_grad], 2)
    passing = None
    for step in range(1, depth + 1):
        dz = step % depth
        value = both_grad[:, dz * block_rows : (dz + 1) * block_rows]
        if passing is not None:
            value = value + wide(passing)
        if dz:
            passing = z_shift(low(value))
    value, gate_up_grad = tie(value, gate_up_grad)
    out_parts, value = tie(out_parts, value)
    out_sum = scatter_z(place, out_parts)
    query_raw_grad, query_gain_grad = queries_pull(
        query_grad.reshape(sequences, block_rows, local_heads, HEAD_SIZE)
    )
    keys_raw_grad, key_gain_grad = keys_pull(
        (value[:, :, :local_groups], value[:, :, local_groups:])
    )
    mixed_low = jnp.concatenate([low(query_raw_grad), low(keys_raw_grad)], 1)
    mixed_weight_grad = scatter_z(place, scatter_attention(flat_in, mixed_low))
    block_in_grad = jnp.concatenate(
        [matmul_t(mixed_low, mixed_near), matmul_t(mixed_low, mixed_far)], 1
    ).reshape(sequences, block_rows, width)
    block_in_sum = place.move(
        sum_two(block_in_grad).reshape(-1, width), place.near_to_whole
    ).reshape(shape)
    normed_grad = normed_grad_first + normed_grad_second + block_in_sum
    inputs_grad_second, input_gain_grad = input_pull(normed_grad)
    tokens_grad = inputs_grad_first + inputs_grad_second
    gain_grads = (
        jnp.stack(
            [
                input_gain_grad,
                laurel_gain_grad,
                attention_gain_grad,
                hidden_in_gain_grad,
                hidden_out_gain_grad,
                side_gain_grad,
            ]
        )
    )
    head_grads = jnp.concatenate(
        [query_gain_grad, key_gain_grad, jnp.zeros((width - 2 * HEAD_SIZE,), jnp.float32)]
    )
    gain_grads = sum_everywhere(place, jnp.concatenate([gain_grads, head_grads[None]], 0))
    gain_grads = tuple(gain_grads[:6]) + (
        gain_grads[6, :HEAD_SIZE],
        gain_grads[6, HEAD_SIZE : 2 * HEAD_SIZE],
    )
    gate_grad, up_grad = join_four(place, wide(gate_up_grad), 2)
    kept, sent = halves_of(
        jnp.concatenate([out_sum[:, query_width:], wide(side_grads)], 1), 0, place.y
    )
    small_grads = kept + wide(y_swap(low(sent)))
    side_input_grad = side_input_grad.reshape(sequences, own_rows, side_width)
    return (
        (result, tokens_grad, side_input_grad)
        + (
            mixed_weight_grad[:, :query_width],
            mixed_weight_grad[:, query_width : query_width + key_width],
            mixed_weight_grad[:, query_width + key_width :],
            out_sum[:, :query_width].T,
            gate_grad,
            up_grad,
            down_grad_t.T,
        )
        + (
            small_grads[:, :rank],
            small_grads[:, rank : 2 * rank].T,
            small_grads[:, 2 * rank : 2 * rank + side_width],
            small_grads[:, 2 * rank + side_width :].T,
        )
        + gain_grads
    )


def solution(mesh):
    sizes = (mesh.shape["fsdp"] // 2, 2, mesh.shape["ctx"] // 2, 2, mesh.shape["tp"])
    mesh = Mesh(mesh.devices.reshape(sizes), ("x", "core", "pair", "odd", "tp"))
    placed = (
        P(("x", "core"), ("pair", "odd", "tp"), None),
        P(("x", "core"), ("pair", "odd", "tp"), None),
        P(("x", "core")),
        P(("x", "core"), ("pair", "odd")),
        P(("x", "core"), ("pair", "odd", "tp"), None),
        P(("x", "core", "pair", "odd"), "tp"),
        P(("x", "core", "pair", "odd"), "tp"),
        P(("x", "core", "pair", "odd"), "tp"),
        P("tp", ("x", "core", "pair", "odd")),
        P(("x", "core", "pair", "odd"), "tp"),
        P(("x", "core", "pair", "odd"), "tp"),
        P("tp", ("x", "core", "pair", "odd")),
        P(("x", "core", "pair", "odd", "tp"), None),
        P(None, ("x", "core", "pair", "odd", "tp")),
        P(("x", "core", "pair", "odd", "tp"), None),
        P(None, ("x", "core", "pair", "odd", "tp")),
        P(),
        P(),
        P(),
        P(),
        P(),
        P(),
        P(),
        P(),
    )
    return jax.shard_map(
        on_device,
        mesh=mesh,
        in_specs=placed,
        out_specs=(
            P(("x", "core"), ("pair", "odd", "tp"), None),
            P(("x", "core"), ("pair", "odd", "tp"), None),
            P(("x", "core"), ("pair", "odd", "tp"), None),
            P(("x", "core", "pair", "odd"), "tp"),
            P(("x", "core", "pair", "odd"), "tp"),
            P(("x", "core", "pair", "odd"), "tp"),
            P("tp", ("x", "core", "pair", "odd")),
            P(("x", "core", "pair", "odd"), "tp"),
            P(("x", "core", "pair", "odd"), "tp"),
            P("tp", ("x", "core", "pair", "odd")),
            P(("x", "core", "pair", "odd", "tp"), None),
            P(None, ("x", "core", "pair", "odd", "tp")),
            P(("x", "core", "pair", "odd", "tp"), None),
            P(None, ("x", "core", "pair", "odd", "tp")),
            P(),
            P(),
            P(),
            P(),
            P(),
            P(),
            P(),
            P(),
        ),
        check_vma=False,
    )
```

```python
import jax
import jax.numpy as jnp
from jax import lax
from jax.experimental import pallas as pl
from jax.experimental.pallas import tpu as pltpu
from jax.sharding import Mesh, PartitionSpec as P

HEAD_SIZE = 256


EPS = 1e-06
THETA = 1000000.0
MASKED = -1e30
SQRT_HALF = 0.7071067811865476
LANES = 128


def scaled_norm(value, gain):
    return value * lax.rsqrt(jnp.mean(value * value, axis=-1, keepdims=True) + EPS) * gain


def plain_norm(value):
    return value * lax.rsqrt(jnp.mean(value * value, axis=-1, keepdims=True) + EPS)


def rotate(value, cosine, sine):
    half = value.shape[-1] // 2
    first = value[..., :half]
    second = value[..., half:]
    return jnp.concatenate(
        [first * cosine - second * sine, second * cosine + first * sine], axis=-1
    )


def geglu(gate, upward):
    return jax.nn.gelu(gate, approximate=True) * upward


def attention_mix(inputs, attention, normed, laurel, attention_gain, laurel_gain):
    return (
        inputs + scaled_norm(attention, attention_gain) + normed + scaled_norm(laurel, laurel_gain)
    ) * SQRT_HALF


def residual_mix(residual, branch, gain):
    return residual + scaled_norm(branch, gain)


def matmul(left, right):
    return jnp.dot(left, right, preferred_element_type=jnp.float32)


def matmul_t(left, right):
    return lax.dot_general(
        left, right, (((1,), (1,)), ((), ())), preferred_element_type=jnp.float32
    )


def low(value):
    return value.astype(jnp.bfloat16)


def wide(value):
    return value.astype(jnp.float32)


def tie(*values):
    return lax.optimization_barrier(values)


CTX = ("pair", "odd")


def core_swap(value):
    return lax.ppermute(value, "core", [(0, 1), (1, 0)])


def x_shift(value, step=1):
    size = lax.axis_size("x")
    return lax.ppermute(value, "x", [(i, (i + step) % size) for i in range(size)])


def z_shift(value, step=1):
    size = lax.axis_size(CTX)
    return lax.ppermute(value, CTX, [(i, (i + step) % size) for i in range(size)])


def pair_shift(value):
    size = lax.axis_size("pair")
    return lax.ppermute(value, "pair", [(i, (i + 1) % size) for i in range(size)])


def odd_swap(value):
    return lax.ppermute(value, "odd", [(0, 1), (1, 0)])


def y_swap(value):
    return lax.ppermute(value, "tp", [(0, 1), (1, 0)])


def in_order(own, mine, other, axis):
    first = jnp.where(own == 0, mine, other)
    second = jnp.where(own == 0, other, mine)
    return jnp.stack([first, second], axis)


def halves_of(value, axis, own):
    shape = value.shape
    value = value.reshape(shape[:axis] + (2, shape[axis] // 2) + shape[axis + 1 :])
    kept = lax.dynamic_index_in_dim(value, own, axis, False)
    return kept, lax.dynamic_index_in_dim(value, 1 - own, axis, False)


class Place:
    def __init__(self, rows):
        self.rows = rows
        self.chips = chips = lax.axis_size("x")
        self.pairs = pairs = lax.axis_size("pair")
        self.depth = depth = 2 * pairs
        self.core = core = lax.axis_index("core")
        self.x = x = lax.axis_index("x")
        self.y = lax.axis_index("tp")
        self.pair = pair = lax.axis_index("pair")
        self.odd = lax.axis_index("odd")
        self.z = z = pair * 2 + self.odd
        count = 2 * chips * depth

        def whole(xs, cores, zs):
            return (xs * 2 + cores) * depth + zs

        def near(xs, cores, zs):
            return (((core + cores) % 2) * chips + (x - xs) % chips) * depth + (z - zs) % depth

        at = jnp.arange(count, dtype=jnp.int32)
        of_whole = (at // (2 * depth), (at // depth) % 2, at % depth)
        of_near = (
            (x - (at // depth) % chips) % chips,
            (core + at // (chips * depth)) % 2,
            (z - at) % depth,
        )
        self.whole_to_near = whole(*of_near).astype(jnp.int32)
        self.near_to_whole = near(*of_whole).astype(jnp.int32)

    def move(self, value, index):
        rows = self.rows
        if rows % LANES:
            shape = value.shape
            value = value.reshape(shape[0], -1, rows)
            return jnp.take(value, index, axis=1).reshape(shape)

        def kernel(index_ref, value_ref, out_ref):
            for i in range(value.shape[1] // rows):
                start = pl.multiple_of(index_ref[i] * rows, LANES)
                out_ref[:, i * rows : (i + 1) * rows] = value_ref[:, pl.ds(start, rows)]

        return pl.pallas_call(
            kernel,
            out_shape=jax.ShapeDtypeStruct(value.shape, value.dtype),
            in_specs=[
                pl.BlockSpec(memory_space=pltpu.SMEM),
                pl.BlockSpec(memory_space=pltpu.VMEM),
            ],
            out_specs=pl.BlockSpec(memory_space=pltpu.VMEM),
            name="move_blocks",
        )(index, value)


def z_ring(place, shard):
    ring = [shard]
    for _ in range(1, place.depth):
        ring.append(z_shift(ring[-1]))
    return ring


def rows_of(place, columns):
    return jnp.concatenate(
        [column[dx] for dx in range(place.chips) for column in columns], 0
    )


def scatter_x(place, partial, splits):
    rows = place.rows
    parts = {}
    for first, last in splits:
        run = None
        for dx in range(1, place.chips):
            value = partial(dx, first, last)
            if run is not None:
                value = value + wide(run)
            run = x_shift(low(value))
        value = partial(0, first, last)
        if run is not None:
            value = value + wide(run)
        for dz in range(first, last):
            parts[dz] = value[(dz - first) * rows : (dz - first + 1) * rows]
    return parts


def scatter_z(place, parts):
    passing = None
    for step in range(1, place.depth):
        value = parts[step]
        if passing is not None:
            value = value + wide(passing)
        passing = z_shift(low(value))
    return parts[0] + wide(passing)


def sum_everywhere(place, value):
    value = value + core_swap(value)
    value = value + y_swap(value)
    value = sum([x_shift(value, step) for step in range(1, place.chips)], value)
    return sum([z_shift(value, step) for step in range(1, place.depth)], value)


def swap_middle(place, value, first):
    second = 2 * place.pairs // first
    size = 2 * place.rows
    return jnp.concatenate(
        [
            value[:, ((x * first + a) * second + b) * size :][:, :size]
            for x in range(place.chips)
            for b in range(second)
            for a in range(first)
        ],
        1,
    )


def to_fixed(place, value):
    return swap_middle(place, value, 2)


def from_fixed(place, value):
    return swap_middle(place, value, place.pairs)


def take(value, index, axis):
    return lax.dynamic_index_in_dim(value, index, axis, False)


def quarters(place, shards):
    return jnp.concatenate([shard.reshape(place.rows, 2, 2, -1) for shard in shards], 3)


def join_four(place, value, parts):
    rows = place.rows
    value = value.reshape(2, 2, rows, -1)
    kept = lax.dynamic_index_in_dim(value, place.odd, 1, False)
    sent = lax.dynamic_index_in_dim(value, 1 - place.odd, 1, False)
    value = in_order(place.odd, kept, wide(odd_swap(low(sent))), 2)
    kept = lax.dynamic_index_in_dim(value, place.core, 0, False)
    sent = lax.dynamic_index_in_dim(value, 1 - place.core, 0, False)
    value = in_order(place.core, kept, core_swap(sent), 1)
    return [part.reshape(rows, -1) for part in jnp.split(value, parts, 3)]


def x_ring(place, piece):
    pieces = [piece]
    for _ in range(1, place.chips):
        pieces.append(x_shift(pieces[-1]))
    return pieces


def share_four(value):
    half = value.shape[0] // 2
    beside = y_swap(value)
    above = odd_swap(value)
    across = [y_swap(above[:half]), odd_swap(beside[half:])]
    return jnp.concatenate([value, beside, above] + across, 0)


def add_core(value):
    return jnp.concatenate([value, core_swap(value)], 0)


def sum_across(value, arrived, product):
    rows = value.shape[0] // 8
    half = rows // 2

    def own(first, last):
        return product(value[first:last]) + wide(arrived[first:last])

    across = low(own(3 * rows, 4 * rows))
    above_half = y_swap(across[:half])
    beside_half = odd_swap(across[half:])
    beside_first = y_swap(low(own(rows, rows + half)))
    above_last = odd_swap(low(own(2 * rows + half, 3 * rows)))
    return own, across, above_half, beside_half, beside_first, above_last


def sum_beside(rows, own, above_half, beside_half):
    half = rows // 2
    beside_last = y_swap(low(own(rows + half, 2 * rows) + wide(beside_half)))
    above_first = odd_swap(low(own(2 * rows, 2 * rows + half) + wide(above_half)))
    return beside_last, above_first


def add_halves(value, beside, above):
    half = value.shape[0] // 2
    return jnp.concatenate(
        [
            value[part * half : (part + 1) * half] + wide(beside[part]) + wide(above[part])
            for part in range(2)
        ],
        0,
    )


def share_two(value):
    return jnp.concatenate([value, y_swap(value)], 1)


def sum_two(value):
    rows = value.shape[1] // 2
    return value[:, :rows] + wide(y_swap(low(value[:, rows:])))


GELU_SCALE = 0.7978845608028654
GELU_CUBE = 0.044715


def gelu_parts(gate):
    square = gate * gate
    bend = jnp.tanh(GELU_SCALE * gate * (1.0 + GELU_CUBE * square))
    half = 0.5 + 0.5 * bend
    slope = half + 0.5 * gate * (1.0 - bend * bend) * (
        GELU_SCALE * (1.0 + 3.0 * GELU_CUBE * square)
    )
    return gate * half, slope


def hidden_backward(block, weights, both):
    rows, width = block.shape
    units = weights.shape[1]
    tile, chunk = min(1024, rows), min(256, units)

    def kernel(block_ref, weights_ref, both_ref, out_ref):
        for start in range(0, units, chunk):
            grad = jnp.dot(
                block_ref[...],
                weights_ref[:, start : start + chunk],
                preferred_element_type=jnp.float32,
            )
            value, slope = gelu_parts(both_ref[:, start : start + chunk])
            up = both_ref[:, units + start : units + start + chunk]
            out_ref[:, start : start + chunk] = (grad * up * slope).astype(jnp.bfloat16)
            out_ref[:, units + start : units + start + chunk] = (grad * value).astype(
                jnp.bfloat16
            )

    return pl.pallas_call(
        kernel,
        grid=(rows // tile,),
        in_specs=[
            pl.BlockSpec((tile, width), lambda i: (i, 0)),
            pl.BlockSpec((width, units), lambda i: (0, 0)),
            pl.BlockSpec((tile, 2 * units), lambda i: (i, 0)),
        ],
        out_specs=pl.BlockSpec((tile, 2 * units), lambda i: (i, 0)),
        out_shape=jax.ShapeDtypeStruct((rows, 2 * units), jnp.bfloat16),
        compiler_params=pltpu.CompilerParams(vmem_limit_bytes=56 * 2**20),
        cost_estimate=pl.CostEstimate(
            flops=2 * rows * width * units,
            transcendentals=rows * units,
            bytes_accessed=2 * rows * width + 2 * width * units + 12 * rows * units,
        ),
        name="hidden_backward",
    )(block, weights, both)


def on_device(
    tokens,
    side_input,
    prefix,
    positions,
    cotangent,
    query_weight,
    key_matrix,
    value_matrix,
    out_weight,
    gate_weight,
    up_weight,
    down_weight,
    laurel_left,
    laurel_right,
    side_gate_weight,
    side_out_weight,
    input_gain,
    laurel_gain,
    attention_gain,
    hidden_in_gain,
    hidden_out_gain,
    side_gain,
    query_gain,
    key_gain,
):
    shard_rows = query_weight.shape[0]
    place = Place(shard_rows)
    chips, depth = place.chips, place.depth
    sequences, own_rows, width = tokens.shape
    shape = tokens.shape
    side_width = side_input.shape[2]
    rank = laurel_left.shape[1]
    block_rows = positions.shape[1]
    query_width = query_weight.shape[1]
    key_width = key_matrix.shape[1]
    hidden_part = gate_weight.shape[1] // 4
    local_heads = query_width // HEAD_SIZE
    local_groups = key_width // HEAD_SIZE
    per_group = local_heads // local_groups

    near_rows = place.y * own_rows + jnp.arange(own_rows, dtype=jnp.int32)
    far_rows = (1 - place.y) * own_rows + jnp.arange(own_rows, dtype=jnp.int32)
    block_index = jnp.concatenate([near_rows, far_rows])
    row_index = place.z * block_rows + block_index
    near_positions = lax.dynamic_slice_in_dim(positions, place.y * own_rows, own_rows, 1)
    far_positions = lax.dynamic_slice_in_dim(positions, (1 - place.y) * own_rows, own_rows, 1)
    positions = jnp.concatenate([near_positions, far_positions], 1)
    freq = THETA ** (
        -(jnp.arange(HEAD_SIZE // 2, dtype=jnp.float32) * 2.0) / HEAD_SIZE
    )
    angle = positions.astype(jnp.float32)[..., None] * freq
    cosine = jnp.cos(angle)[..., None, :]
    sine = jnp.sin(angle)[..., None, :]

    inputs = tokens.astype(jnp.float32)
    normed, input_pull = jax.vjp(scaled_norm, inputs, input_gain)
    normed_reduced = normed.astype(jnp.bfloat16)
    flat_normed = normed_reduced.reshape(-1, width)
    half_width = width // 2
    everywhere = ("x", "core", "pair", "odd", "tp")

    small = jnp.concatenate(
        [laurel_left, laurel_right.T, side_gate_weight, side_out_weight.T], 1
    )
    small_full = lax.all_gather(small, everywhere, axis=0, tiled=True)
    out_shard, small_full = tie(out_weight.T, small_full)
    out_full = lax.all_gather(out_shard, everywhere[:4], axis=0, tiled=True)
    laurel_down = small_full[:, :rank]
    laurel_up_t = small_full[:, rank : 2 * rank]
    side_gate_full = small_full[:, 2 * rank : 2 * rank + side_width]
    side_out_t = small_full[:, 2 * rank + side_width :]

    mixed_shard = jnp.concatenate([query_weight, key_matrix, value_matrix], 1)
    gate_up = quarters(place, [gate_weight, up_weight])
    gate_up_arrived = odd_swap(take(gate_up, 1 - place.odd, 2))
    down = quarters(place, [down_weight.T])
    down_arrived = core_swap(take(down, 1 - place.core, 1))
    mixed_ring = [mixed_shard, z_shift(mixed_shard)]
    mixed_columns = [x_ring(place, mixed_shard)]
    down = in_order(place.core, take(down, place.core, 1), down_arrived, 0)
    down_kept, down_sent = take(down, place.odd, 2), take(down, 1 - place.odd, 2)
    near_in = place.move(flat_normed, place.whole_to_near).reshape(shape)
    near_in, mixed_ring[-1] = tie(near_in, mixed_ring[-1])
    flat_in = share_two(near_in)
    for step in range(2, depth):
        mixed_ring.append(z_shift(mixed_ring[-1]))
        mixed_columns.append(x_ring(place, mixed_ring[-2]))
        mixed_ring[-1], mixed_columns[-2] = tie(mixed_ring[-1], mixed_columns[-2])
        if step == 2:
            mixed_ring[-1], gate_up_arrived, down_kept, down_sent = tie(
                mixed_ring[-1], gate_up_arrived, down_kept, down_sent
            )
            down_arrived = odd_swap(down_sent)
    gate_up = in_order(place.odd, take(gate_up, place.odd, 2), gate_up_arrived, 0)
    gate_up_kept = take(gate_up, place.core, 2)
    gate_up_arrived = core_swap(take(gate_up, 1 - place.core, 2))
    mixed_ring[-1], mixed_columns[-1], flat_in, gate_up_arrived = tie(
        mixed_ring[-1], mixed_columns[-1], flat_in, gate_up_arrived
    )
    flat_in = flat_in.reshape(-1, width)
    mixed_columns.append(x_ring(place, mixed_ring[-1]))
    gate_up_shard = in_order(place.core, gate_up_kept, gate_up_arrived, 0).reshape(
        4 * shard_rows, -1
    )

    mixed_near = rows_of(place, mixed_columns)
    mixed_near, gate_up_shard, down_arrived = tie(mixed_near, gate_up_shard, down_arrived)
    mixed_far = core_swap(mixed_near)
    gate_up_shard, out_full = tie(gate_up_shard, out_full)
    gate_up_full = lax.all_gather(gate_up_shard, ("x", "pair"), axis=0, tiled=True)
    down_shard = in_order(place.odd, down_kept, down_arrived, 1).reshape(4 * shard_rows, -1)
    down_shard, gate_up_full = tie(down_shard, gate_up_full)
    down_full_t = lax.all_gather(down_shard, ("x", "pair"), axis=0, tiled=True)
    def project(first, last):
        return matmul(flat_in[:, :half_width], mixed_near[:, first:last]) + matmul(
            flat_in[:, half_width:], mixed_far[:, first:last]
        )

    key_value_raw = project(query_width, query_width + 2 * key_width)
    query_raw = project(0, query_width)

    def queries_of(part, gain):
        part = part.reshape(sequences, block_rows, local_heads, HEAD_SIZE)
        return rotate(scaled_norm(part, gain), cosine, sine)

    def keys_of(part, gain):
        keys = part[:, :key_width].reshape(sequences, block_rows, local_groups, HEAD_SIZE)
        values = part[:, key_width:].reshape(sequences, block_rows, local_groups, HEAD_SIZE)
        return rotate(scaled_norm(keys, gain), cosine, sine), plain_norm(values)

    (keys, values), keys_pull = jax.vjp(keys_of, key_value_raw, key_gain)
    query_rows, queries_pull = jax.vjp(queries_of, query_raw, query_gain)
    query_low = query_rows.astype(jnp.bfloat16).reshape(
        sequences, block_rows, local_groups, per_group, HEAD_SIZE
    )
    both = jnp.concatenate([low(keys), low(values)], 2)
    pieces = z_ring(place, both)
    key_index = jnp.concatenate(
        [((place.z - dz) % depth) * block_rows + block_index for dz in range(depth)]
    )
    everyone = jnp.concatenate(pieces, 1)
    all_keys = everyone[:, :, :local_groups]
    all_values = everyone[:, :, local_groups:]
    visible = (key_index[None, None, :] <= row_index[None, :, None]) | (
        key_index[None, None, :] < prefix[:, None, None]
    )

    def all_scores():
        scores = jnp.einsum(
            "sbkgd,sjkd->skgbj", query_low, all_keys, preferred_element_type=jnp.float32
        )
        return jnp.where(visible[:, None, None], scores, MASKED)

    scores = all_scores()
    highest = jnp.max(scores, axis=-1, keepdims=True)
    log_total = highest + jnp.log(jnp.sum(jnp.exp(scores - highest), axis=-1, keepdims=True))
    probs = jnp.exp(scores - log_total)
    probs_low = low(probs)
    attended = jnp.einsum(
        "skgbj,sjkd->sbkgd", probs_low, all_values, preferred_element_type=jnp.float32
    )
    attended_low = attended.astype(jnp.bfloat16).reshape(
        sequences * block_rows, local_heads * HEAD_SIZE
    )
    attention = sum_two(matmul_t(attended_low, out_full).reshape(sequences, block_rows, width))
    laurel_mid = matmul(flat_normed, laurel_down).astype(jnp.bfloat16)
    laurel_out = matmul_t(laurel_mid, laurel_up_t).reshape(shape)
    mixed, mix_pull = jax.vjp(
        attention_mix, inputs, attention, normed, laurel_out, attention_gain, laurel_gain
    )
    hidden_in, pre_pull = jax.vjp(scaled_norm, mixed, hidden_in_gain)
    hidden_block = share_four(
        to_fixed(place, low(hidden_in).reshape(-1, width))
    )

    hidden_block = add_core(hidden_block)
    gate_up_out = matmul(hidden_block, gate_up_full)
    hidden_low = low(geglu(gate_up_out[:, :hidden_part], gate_up_out[:, hidden_part:]))
    token_rows = sequences * own_rows

    def down_product(value):
        return matmul_t(value, down_full_t)

    far_out = low(down_product(hidden_low[4 * token_rows :]))
    own, _, above_half, beside_half, beside_first, above_last = sum_across(
        hidden_low, core_swap(far_out), down_product
    )
    beside_last, above_first = sum_beside(token_rows, own, above_half, beside_half)
    hidden_out = add_halves(
        own(0, token_rows), (beside_first, beside_last), (above_first, above_last)
    )
    hidden_out = from_fixed(place, hidden_out).reshape(shape)
    layer_out, post_pull = jax.vjp(residual_mix, mixed, hidden_out, hidden_out_gain)
    layer_low = layer_out.astype(jnp.bfloat16).reshape(-1, width)
    side_pre = matmul(layer_low, side_gate_full)
    side_act, side_pull = jax.vjp(
        geglu, side_pre, side_input.astype(jnp.float32).reshape(-1, side_width)
    )
    side_low = side_act.astype(jnp.bfloat16)
    projected = matmul_t(side_low, side_out_t).reshape(shape)
    result, final_pull = jax.vjp(residual_mix, layer_out, projected, side_gain)
    result = low(result)
    out_grad_first, projected_grad, side_gain_grad = final_pull(cotangent.astype(jnp.float32))
    projected_low = projected_grad.astype(jnp.bfloat16).reshape(-1, width)
    side_out_grad_t = matmul(projected_low.T, side_low)
    side_grad = matmul(projected_low, side_out_t)
    side_pre_grad, side_input_grad = side_pull(side_grad)
    side_pre_low = side_pre_grad.astype(jnp.bfloat16)
    side_gate_grad = matmul(layer_low.T, side_pre_low)
    layer_grad = out_grad_first + matmul_t(side_pre_low, side_gate_full).reshape(shape)
    mixed_grad_first, hidden_out_grad, hidden_out_gain_grad = post_pull(layer_grad)
    hidden_out_block = add_core(
        share_four(to_fixed(place, low(hidden_out_grad).reshape(-1, width)))
    )

    side_grads = lax.psum_scatter(
        low(jnp.concatenate([side_gate_grad, side_out_grad_t], 1)),
        everywhere[:4],
        scatter_dimension=0,
        tiled=True,
    )
    down_grad = low(matmul(hidden_out_block.T, hidden_low))
    hidden_out_block, down_grad = tie(hidden_out_block, down_grad)
    down_grad, side_grads = tie(down_grad, side_grads)
    down_grad = lax.psum_scatter(down_grad, ("x", "pair"), scatter_dimension=0, tiled=True)
    gate_up_low = hidden_backward(hidden_out_block, down_full_t, gate_up_out)

    def gate_up_product(value):
        return matmul_t(value, gate_up_full)

    far_out = low(gate_up_product(gate_up_low[4 * token_rows :]))
    own, across, above_half, beside_half, beside_first, above_last = sum_across(
        gate_up_low, core_swap(far_out), gate_up_product
    )
    wgrad_low, across = tie(gate_up_low, across)
    gate_up_grad = low(matmul(hidden_block.T, wgrad_low))
    beside_last, above_first = sum_beside(token_rows, own, above_half, beside_half)
    hidden_in_sum = own(0, token_rows)
    hidden_in_sum, gate_up_grad = tie(hidden_in_sum, gate_up_grad)
    hidden_in_sum = add_halves(
        hidden_in_sum, (beside_first, beside_last), (above_first, above_last)
    )
    hidden_in_sum = from_fixed(place, hidden_in_sum).reshape(shape)
    gate_up_grad = lax.psum_scatter(
        gate_up_grad, ("x", "pair"), scatter_dimension=0, tiled=True
    )
    mixed_grad_second, hidden_in_gain_grad = pre_pull(hidden_in_sum)
    mixed_grad = mixed_grad_first + mixed_grad_second
    (
        inputs_grad_first,
        attention_grad,
        normed_grad_first,
        laurel_grad,
        attention_gain_grad,
        laurel_gain_grad,
    ) = mix_pull(mixed_grad)
    attention_grad, down_grad = tie(attention_grad, down_grad)
    attention_block = share_two(low(attention_grad)).reshape(-1, width)
    (down_grad_t,) = join_four(place, wide(down_grad), 1)

    attended_grad = (
        matmul(attention_block, out_full)
        .astype(jnp.bfloat16)
        .reshape(sequences, block_rows, local_groups, per_group, HEAD_SIZE)
    )
    laurel_low = laurel_grad.astype(jnp.bfloat16).reshape(-1, width)
    laurel_mid_grad = matmul(laurel_low, laurel_up_t).astype(jnp.bfloat16)
    normed_grad_second = matmul_t(laurel_mid_grad, laurel_down).reshape(shape)

    def scatter_attention(left, right, extra=None):
        def rows(start, end):
            value = matmul(left[:, start:end].T, right)
            return value if extra is None else jnp.concatenate([value, extra[start:end]], 1)

        arrived = core_swap(low(rows(half_width, width)))

        def partial(dx, first, last):
            start, end = (dx * depth + first) * shard_rows, (dx * depth + last) * shard_rows
            return rows(start, end) + wide(arrived[start:end])

        return scatter_x(place, partial, [(1, depth), (0, 1)])

    near_own = near_in.reshape(-1, width)
    laurel_near = place.move(laurel_low, place.whole_to_near)
    out_parts = scatter_attention(
        place.move(attention_block, place.whole_to_near),
        attended_low,
        jnp.concatenate(
            [matmul(near_own.T, laurel_mid_grad), matmul(laurel_near.T, laurel_mid)], 1
        ),
    )

    delta = jnp.transpose(
        jnp.sum(attended_grad.astype(jnp.float32) * attended, axis=-1), (0, 2, 3, 1)
    )
    probs = jnp.exp(all_scores() - log_total)
    probs_grad = jnp.einsum(
        "sbkgd,sjkd->skgbj", attended_grad, all_values, preferred_element_type=jnp.float32
    )
    scores_grad = low(probs * (probs_grad - delta[..., None]))
    query_grad = jnp.einsum(
        "skgbj,sjkd->sbkgd", scores_grad, all_keys, preferred_element_type=jnp.float32
    )
    keys_grad = jnp.einsum(
        "skgbj,sbkgd->sjkd", scores_grad, query_low, preferred_element_type=jnp.float32
    )
    values_grad = jnp.einsum(
        "skgbj,sbkgd->sjkd", low(probs), attended_grad, preferred_element_type=jnp.float32
    )
    both_grad = jnp.concatenate([keys_grad, values_grad], 2)
    passing = None
    for step in range(1, depth + 1):
        dz = step % depth
        value = both_grad[:, dz * block_rows : (dz + 1) * block_rows]
        if passing is not None:
            value = value + wide(passing)
        if dz:
            passing = z_shift(low(value))
    value, gate_up_grad = tie(value, gate_up_grad)
    out_parts, value = tie(out_parts, value)
    out_sum = scatter_z(place, out_parts)
    query_raw_grad, query_gain_grad = queries_pull(
        query_grad.reshape(sequences, block_rows, local_heads, HEAD_SIZE)
    )
    keys_raw_grad, key_gain_grad = keys_pull(
        (value[:, :, :local_groups], value[:, :, local_groups:])
    )
    mixed_low = jnp.concatenate([low(query_raw_grad), low(keys_raw_grad)], 1)
    mixed_weight_grad = scatter_z(place, scatter_attention(flat_in, mixed_low))
    block_in_grad = jnp.concatenate(
        [matmul_t(mixed_low, mixed_near), matmul_t(mixed_low, mixed_far)], 1
    ).reshape(sequences, block_rows, width)
    block_in_sum = place.move(
        sum_two(block_in_grad).reshape(-1, width), place.near_to_whole
    ).reshape(shape)
    normed_grad = normed_grad_first + normed_grad_second + block_in_sum
    inputs_grad_second, input_gain_grad = input_pull(normed_grad)
    tokens_grad = inputs_grad_first + inputs_grad_second
    gain_grads = (
        jnp.stack(
            [
                input_gain_grad,
                laurel_gain_grad,
                attention_gain_grad,
                hidden_in_gain_grad,
                hidden_out_gain_grad,
                side_gain_grad,
            ]
        )
    )
    head_grads = jnp.concatenate(
        [query_gain_grad, key_gain_grad, jnp.zeros((width - 2 * HEAD_SIZE,), jnp.float32)]
    )
    gain_grads = sum_everywhere(place, jnp.concatenate([gain_grads, head_grads[None]], 0))
    gain_grads = tuple(gain_grads[:6]) + (
        gain_grads[6, :HEAD_SIZE],
        gain_grads[6, HEAD_SIZE : 2 * HEAD_SIZE],
    )
    gate_grad, up_grad = join_four(place, wide(gate_up_grad), 2)
    kept, sent = halves_of(
        jnp.concatenate([out_sum[:, query_width:], wide(side_grads)], 1), 0, place.y
    )
    small_grads = kept + wide(y_swap(low(sent)))
    side_input_grad = side_input_grad.reshape(sequences, own_rows, side_width)
    return (
        (result, tokens_grad, side_input_grad)
        + (
            mixed_weight_grad[:, :query_width],
            mixed_weight_grad[:, query_width : query_width + key_width],
            mixed_weight_grad[:, query_width + key_width :],
            out_sum[:, :query_width].T,
            gate_grad,
            up_grad,
            down_grad_t.T,
        )
        + (
            small_grads[:, :rank],
            small_grads[:, rank : 2 * rank].T,
            small_grads[:, 2 * rank : 2 * rank + side_width],
            small_grads[:, 2 * rank + side_width :].T,
        )
        + gain_grads
    )


def solution(mesh):
    sizes = (mesh.shape["fsdp"] // 2, 2, mesh.shape["ctx"] // 2, 2, mesh.shape["tp"])
    mesh = Mesh(mesh.devices.reshape(sizes), ("x", "core", "pair", "odd", "tp"))
    placed = (
        P(("x", "core"), ("pair", "odd", "tp"), None),
        P(("x", "core"), ("pair", "odd", "tp"), None),
        P(("x", "core")),
        P(("x", "core"), ("pair", "odd")),
        P(("x", "core"), ("pair", "odd", "tp"), None),
        P(("x", "core", "pair", "odd"), "tp"),
        P(("x", "core", "pair", "odd"), "tp"),
        P(("x", "core", "pair", "odd"), "tp"),
        P("tp", ("x", "core", "pair", "odd")),
        P(("x", "core", "pair", "odd"), "tp"),
        P(("x", "core", "pair", "odd"), "tp"),
        P("tp", ("x", "core", "pair", "odd")),
        P(("x", "core", "pair", "odd", "tp"), None),
        P(None, ("x", "core", "pair", "odd", "tp")),
        P(("x", "core", "pair", "odd", "tp"), None),
        P(None, ("x", "core", "pair", "odd", "tp")),
        P(),
        P(),
        P(),
        P(),
        P(),
        P(),
        P(),
        P(),
    )
    return jax.shard_map(
        on_device,
        mesh=mesh,
        in_specs=placed,
        out_specs=(
            P(("x", "core"), ("pair", "odd", "tp"), None),
            P(("x", "core"), ("pair", "odd", "tp"), None),
            P(("x", "core"), ("pair", "odd", "tp"), None),
            P(("x", "core", "pair", "odd"), "tp"),
            P(("x", "core", "pair", "odd"), "tp"),
            P(("x", "core", "pair", "odd"), "tp"),
            P("tp", ("x", "core", "pair", "odd")),
            P(("x", "core", "pair", "odd"), "tp"),
            P(("x", "core", "pair", "odd"), "tp"),
            P("tp", ("x", "core", "pair", "odd")),
            P(("x", "core", "pair", "odd", "tp"), None),
            P(None, ("x", "core", "pair", "odd", "tp")),
            P(("x", "core", "pair", "odd", "tp"), None),
            P(None, ("x", "core", "pair", "odd", "tp")),
            P(),
            P(),
            P(),
            P(),
            P(),
            P(),
            P(),
            P(),
        ),
        check_vma=False,
    )
```
